32 devices in a mesh: pipe: 4 (over x, core), expert: 2 (over y), dp: 4 (over z).
Axes of the slice: x: 2, y: 2, z: 4, core: 2. Of those that a mesh axis runs over, the one named last changes fastest.
Arguments:
- acts_fwd: bfloat16 [4, 4, 128, 768], P('pipe', 'dp', 'expert'), may hold values from -6 to 6
- ids_fwd: int32 [4, 4, 128, 2], P('pipe', 'dp', 'expert'), may hold values from 0 to 3, all different within a row; in each aligned block of 64 rows (0 to 63, 64 to 127, ..., all dimensions but the last counted through in order) at most 36 rows name the same one
- norm_gain: float32 [4, 768], P('pipe'), may hold values from 0.1 to 1.9
- router_w: bfloat16 [4, 768, 4], P('pipe'), may hold values from -0.21875 to 0.21875
- gate_w: bfloat16 [4, 4, 768, 1536], P('pipe', 'expert'), may hold values from -0.21875 to 0.21875
- up_w: bfloat16 [4, 4, 768, 1536], P('pipe', 'expert'), may hold values from -0.21875 to 0.21875
- down_w: bfloat16 [4, 4, 1536, 768], P('pipe', 'expert'), may hold values from -0.15625 to 0.15625
- normed_bwd: bfloat16 [4, 4, 128, 768], P('pipe', 'dp', 'expert'), may hold values from -6 to 6
- ids_bwd: int32 [4, 4, 128, 2], P('pipe', 'dp', 'expert'), may hold values from 0 to 3, all different within a row; in each aligned block of 64 rows (0 to 63, 64 to 127, ..., all dimensions but the last counted through in order) at most 36 rows name the same one
- dgate_bwd: bfloat16 [4, 4, 128, 2, 1536], P('pipe', 'dp', 'expert'), may hold values from -0.1875 to 0.1875
Outputs:
- handed_on: bfloat16 [4, 4, 128, 768], P('pipe', 'dp', 'expert')
- grad_gate: float32 [4, 4, 768, 1536], P('pipe', 'expert', 'dp')
The draws below stay inside these ranges and needn't reach their ends.
Inputs may be any that keep to these rules, and one draw needn't show every extreme that they name: `ids_fwd`: each token names two different experts. Among the 64 tokens of one device (aligned blocks of 64 rows in the order section, replica, token) no expert is named more than 36 times, and in every draw some expert is named exactly 36 times in some block. `ids_bwd`: as for ids_fwd.
All inputs are finite; a program needn't handle non-finite values.
Results may differ from the reference program's by a relative error of at most 0.0085.
Values may be sent and summed in bfloat16 or wider, within the bound.
A program may use at most 64 MiB of HBM per device.

```python
import math
import jax
import jax.numpy as jnp
import numpy as np
from jax import lax

D = 768
HID = 1536
EXPERTS = 4
TOK = 64
CAP = 36
MICRO = 128
SECTIONS = 4
REPLICAS = 4


def levels(own_key, extent, cuts, low, top_value):
    gain = 1.0
    for position, shards_of in cuts:
        draws = jax.random.uniform(jax.random.fold_in(jax.random.fold_in(own_key, 6), position), (shards_of,), jnp.float32, low / len(cuts), top_value / len(cuts))
        gain = gain * jnp.repeat(jnp.exp(draws), extent[position] // shards_of).reshape((-1,) + (1,) * (len(extent) - 1 - position))
    return gain


def deal_out(rng, own, number, rows, number_of, top, bound, slope):
    ranking = jax.random.permutation(rng, number_of)
    heavy_load, common = load_shares(number_of, rows * top, bound, slope, True), load_shares(number_of, rows * top, bound, slope, False)
    places = jnp.arange(number_of)

    def named(sizes, turn):
        used = int((sizes > 0).sum())
        fixed = max(1, used // 4)
        passed = fixed + (places - fixed + turn * (used - fixed)) % max(1, number_of - fixed)
        return jnp.zeros((number_of,), jnp.int32).at[ranking[jnp.where(places < fixed, places, passed)]].set(jnp.asarray(sizes, jnp.int32))

    sizes = jnp.where(number % 4 == 0, named(heavy_load, number // 4), named(common, number - number // 4 - 1))
    mixed = jax.random.permutation(jax.random.fold_in(own, 3), number_of)
    donor, receiver = mixed[0:number_of // 2 * 2:2], mixed[1:number_of // 2 * 2:2]
    margin = jnp.minimum(sizes[donor] - 1, bound - sizes[receiver]) // 2
    margin = jnp.where((donor == ranking[0]) | (receiver == ranking[0]) | (sizes[receiver] == 0), 0, jnp.maximum(margin, 0))
    passed = jax.random.randint(jax.random.fold_in(own, 4), (number_of // 2,), 0, 1 << 20) % (margin + 1)
    sizes = sizes.at[donor].add(-passed).at[receiver].add(passed)
    labels = jnp.searchsorted(jnp.cumsum(sizes), jnp.arange(rows * top), side="right").astype(jnp.int32)
    listing = labels.reshape(top, rows).T
    listing = listing[jax.random.permutation(jax.random.fold_in(own, 1), rows)]
    turn = jax.random.randint(jax.random.fold_in(own, 2), (rows, 1), 0, top)
    return jnp.take_along_axis(listing, (jnp.arange(top)[None, :] + turn) % top, axis=1)


def load_shares(number_of, total, reach, slope, full):
    loads = [(1 << 20) // math.isqrt(grade ** slope) + 1 for grade in range(1, number_of + 1)]
    largest = reach if full else min(reach, max(-(-total // number_of), total * loads[0] // sum(loads)))
    least = 1 if total - largest >= number_of - 1 else 0
    holding, rest = [largest] + [least] * (number_of - 1), total - largest - least * (number_of - 1)
    while rest > 0:
        movable = [i for i in range(1, number_of) if holding[i] < largest] or [i for i in range(1, number_of) if holding[i] < reach]
        mass, remaining = sum([loads[i] for i in movable]), rest
        for i in movable:
            more = min(reach - holding[i], max(1, remaining * loads[i] // mass), rest)
            holding[i] = holding[i] + more
            rest = rest - more
    return np.array(holding)


def centred(key, shape, spread, limit, pieces=(), held_as=jnp.bfloat16):
    array = spread * jax.random.normal(key, shape, jnp.float32)
    if pieces:
        array = array * levels(key, shape, pieces, -0.22, 0.18)
    return jnp.clip(array, -limit, limit).astype(held_as)


def setup_inputs(seed: int = 0) -> dict:
    streams_of = jax.random.split(jax.random.key(seed), 11)
    acts_fwd = centred(streams_of[0], (SECTIONS, REPLICAS, MICRO, D), 1.0, 6.0, ((0, 4), (1, 4), (2, 2)))
    ids_fwd_keys = jax.random.split(jax.random.fold_in(streams_of[1], 1), SECTIONS * REPLICAS * MICRO // TOK)
    ids_fwd_turns = jax.random.permutation(jax.random.fold_in(streams_of[1], 3), SECTIONS * REPLICAS * MICRO // TOK)
    ids_fwd = jax.vmap(lambda own, number: deal_out(jax.random.fold_in(streams_of[1], 2), own, number, TOK, EXPERTS, 2, CAP, 1))(ids_fwd_keys, ids_fwd_turns).reshape((SECTIONS, REPLICAS, MICRO, 2))
    norm_gain = jnp.clip(1.0 + 0.18 * jax.random.normal(streams_of[2], (SECTIONS, D), jnp.float32), 0.1, 1.9)
    router_w = centred(streams_of[3], (SECTIONS, D, EXPERTS), D ** -0.5, 0.21875, ((0, 4),))
    gate_w = centred(streams_of[4], (SECTIONS, EXPERTS, D, HID), D ** -0.5, 0.21875, ((0, 4), (1, 2)))
    up_w = centred(streams_of[5], (SECTIONS, EXPERTS, D, HID), D ** -0.5, 0.21875, ((0, 4), (1, 2)))
    down_w = centred(streams_of[6], (SECTIONS, EXPERTS, HID, D), HID ** -0.5, 0.15625, ((0, 4), (1, 2)))
    normed_bwd = centred(streams_of[7], (SECTIONS, REPLICAS, MICRO, D), 1.0, 6.0, ((0, 4), (1, 4), (2, 2)))
    ids_bwd_keys = jax.random.split(jax.random.fold_in(streams_of[8], 1), SECTIONS * REPLICAS * MICRO // TOK)
    ids_bwd_turns = jax.random.permutation(jax.random.fold_in(streams_of[8], 3), SECTIONS * REPLICAS * MICRO // TOK)
    ids_bwd = jax.vmap(lambda own, number: deal_out(jax.random.fold_in(streams_of[8], 2), own, number, TOK, EXPERTS, 2, CAP, 1))(ids_bwd_keys, ids_bwd_turns).reshape((SECTIONS, REPLICAS, MICRO, 2))
    dgate_bwd = centred(streams_of[9], (SECTIONS, REPLICAS, MICRO, 2, HID), 0.03, 0.1875, ((0, 4), (1, 4), (2, 2)))
    return {"acts_fwd": acts_fwd, "ids_fwd": ids_fwd, "norm_gain": norm_gain, "router_w": router_w, "gate_w": gate_w, "up_w": up_w, "down_w": down_w, "normed_bwd": normed_bwd, "ids_bwd": ids_bwd, "dgate_bwd": dgate_bwd}


def rms_norm(row_block, gain_row):
    widened = row_block.astype(jnp.float32)
    inv_scale = lax.rsqrt(lax.optimization_barrier(jnp.mean(widened * widened, axis=-1, keepdims=True)) + 1e-05)
    return (widened * inv_scale * gain_row).astype(jnp.bfloat16)

def section_forward(inputs):
    section_block, chosen, gain_row, router, w_gate, w_up, w_down = inputs
    row_block = section_block.reshape(-1, section_block.shape[-1])
    picked = chosen.reshape(-1, 2)
    normed = rms_norm(row_block, gain_row)
    logits = jnp.dot(normed, router, preferred_element_type=jnp.float32)
    first_logit = jnp.take_along_axis(logits, picked[:, 0:1], axis=1)[:, 0]
    second_logit = jnp.take_along_axis(logits, picked[:, 1:2], axis=1)[:, 0]
    weight_first = jax.nn.sigmoid(first_logit - second_logit)
    weight_second = jax.nn.sigmoid(second_logit - first_logit)
    running = row_block.astype(jnp.float32)
    for expert in range(EXPERTS):
        gate_pre = jnp.dot(normed, w_gate[expert], preferred_element_type=jnp.float32)
        up_pre = jnp.dot(normed, w_up[expert], preferred_element_type=jnp.float32)
        hidden = (jax.nn.gelu(gate_pre) * up_pre).astype(jnp.bfloat16)
        expert_out = jnp.dot(hidden, w_down[expert], preferred_element_type=jnp.float32).astype(jnp.bfloat16)
        expert_out = lax.optimization_barrier(expert_out).astype(jnp.float32)
        coefficient = jnp.where(picked[:, 0] == expert, weight_first, jnp.zeros_like(weight_first))
        coefficient = coefficient + jnp.where(picked[:, 1] == expert, weight_second, jnp.zeros_like(weight_second))
        running = running + coefficient[:, None] * expert_out
    return running.astype(jnp.bfloat16).reshape(section_block.shape)

def section_gradient(inputs):
    normed, chosen, cotangent = inputs
    widened = normed.astype(jnp.float32)
    results = []
    for expert in range(EXPERTS):
        selected = (chosen == expert).astype(jnp.float32)
        folded = lax.optimization_barrier(jnp.sum(selected[..., None] * cotangent.astype(jnp.float32), axis=2))
        term_values = jnp.einsum('rtd,rth->rdh', widened, folded).astype(jnp.bfloat16)
        term_values = lax.optimization_barrier(term_values).astype(jnp.float32)
        results.append(lax.optimization_barrier(jnp.sum(term_values, axis=0)))
    return jnp.stack(results)

def reference(acts_fwd, ids_fwd, norm_gain, router_w, gate_w, up_w, down_w, normed_bwd, ids_bwd, dgate_bwd):
    layer_out = lax.map(section_forward, (acts_fwd, ids_fwd, norm_gain, router_w, gate_w, up_w, down_w))
    handed_on = jnp.roll(layer_out, 1, axis=0)
    gradients = lax.map(section_gradient, (normed_bwd, ids_bwd, dgate_bwd))
    return (handed_on, gradients[::-1])
```

```python
import functools

import jax
import jax.numpy as jnp
from jax import lax
from jax.experimental import pallas as pl
from jax.experimental.pallas import tpu as pltpu
from jax.sharding import PartitionSpec as P

CAP = 36
TILE = 16
CHUNKS = 6
BLOCKS = 3
F32 = jnp.float32
BF16 = jnp.bfloat16


def relay_kernel(
    dims,
    tok_hbm, idf_hbm, gain_hbm, router_hbm, wg_hbm, wu_hbm, wd_hbm, nb_hbm, idb_hbm, dg_hbm,
    ho_ref, grad_ref,
    tok_ref, idf_ref, gain_ref, router_ref, nb_ref, idb_ref, dg_ref, in_sem,
    wg, wu, wd, gs, st, gall, ns, stn, nf, nall, nt, xall, call, hid, acc, ps, rp, mixed, landed,
    w_sem, s1_send, s1_recv, n1_send, n1_recv, z_send, z_recv, nz_send, nz_recv,
    x_send, x_recv, c_send, c_recv, p_send, p_recv, h_sem,
):
    S, G, Z, L = dims
    T, D = tok_ref.shape
    HID = dg_ref.shape[2]
    DZ = D // Z
    HC = HID // CHUNKS
    R = L * CAP
    FR = G * R
    starts = [s * R // TILE * TILE for s in range(G)]
    W = gs.shape[2]
    p = lax.axis_index("pipe")
    e = lax.axis_index("expert")
    d = lax.axis_index("dp")
    mirror = S - 1 - p
    after = lax.rem(p + 1, S)
    before = lax.rem(p + S - 1, S)

    def dev(pp, ee, dd):
        return {"pipe": pp, "expert": ee, "dp": dd}

    def remote(src, dst, ss, rs, to):
        return pltpu.make_async_remote_copy(
            src_ref=src, dst_ref=dst, send_sem=ss, recv_sem=rs,
            device_id=to, device_id_type=pl.DeviceIdType.MESH)

    def local(src, dst, sem):
        return pltpu.make_async_copy(src, dst, sem)

    small = []
    for i, (src, dst) in enumerate((
        (idb_hbm, idb_ref), (dg_hbm, dg_ref), (nb_hbm, nb_ref), (tok_hbm, tok_ref),
        (idf_hbm, idf_ref), (gain_hbm, gain_ref), (router_hbm, router_ref),
    )):
        copy = local(src, dst, in_sem.at[i])
        copy.start()
        small.append(copy)

    weights = []
    for j in range(L):
        trio = [local(wg_hbm.at[j], wg.at[j], w_sem.at[j, 0]),
                local(wu_hbm.at[j], wu.at[j], w_sem.at[j, 1]),
                local(wd_hbm.at[j], wd.at[j], w_sem.at[j, 2])]
        for copy in trio:
            copy.start()
        weights.append(trio)

    barrier = pltpu.get_barrier_semaphore()
    peers = [dev(mirror, g, d) for g in range(G)]
    peers += [dev(p, lax.rem(e + k, G), d) for k in range(1, G)]
    peers += [dev(p, e, lax.rem(d + k, Z)) for k in range(1, Z)]
    peers += [dev(after, e, d), dev(before, e, d)]
    for peer in peers:
        pl.semaphore_signal(barrier, inc=1, device_id=peer, device_id_type=pl.DeviceIdType.MESH)

    small[0].wait()
    ids = [idb_ref[k:k + 1, :].astype(F32) for k in range(2)]
    labels = lax.broadcasted_iota(jnp.int32, (8, T), 0).astype(F32)
    onehot = [jnp.where(ids[k] == labels, 1.0, 0.0) for k in range(2)]
    earlier = lax.broadcasted_iota(jnp.int32, (T, T), 0) < lax.broadcasted_iota(
        jnp.int32, (T, T), 1)
    earlier = jnp.where(earlier, 1.0, 0.0).astype(BF16)
    counts = [jnp.dot(onehot[k].astype(BF16), earlier, preferred_element_type=F32)
              for k in range(2)]
    counts[1] = counts[1] + jnp.sum(onehot[0], axis=1, keepdims=True)
    rank = [jnp.sum(counts[k] * onehot[k], axis=0, keepdims=True) for k in range(2)]
    shift = lax.rem(e * R, TILE).astype(F32)
    slots = lax.broadcasted_iota(jnp.int32, (W, T), 0).astype(F32)
    maps = []
    for g in range(G):
        pair = []
        for k in range(2):
            own = jnp.where((ids[k] >= g * L) & (ids[k] < (g + 1) * L),
                            shift + (ids[k] - g * L) * CAP + rank[k], -1.0)
            pair.append(jnp.where(slots == own, 1.0, 0.0).astype(BF16))
        maps.append(pair)

    stage1 = []
    small[1].wait()
    for c in range(CHUNKS):
        for g in range(G):
            cols = slice(c * HC, (c + 1) * HC)
            gs[g, c] = (
                jnp.dot(maps[g][0], dg_ref[:, 0, cols], preferred_element_type=F32)
                + jnp.dot(maps[g][1], dg_ref[:, 1, cols], preferred_element_type=F32)
            ).astype(BF16)
        if c == 0:
            pl.semaphore_wait(barrier, len(peers))
        for g in range(G):
            copy = remote(gs.at[g, c], st.at[c, e], s1_send.at[c, g], s1_recv.at[c, e],
                          dev(mirror, g, d))
            copy.start()
            stage1.append(copy)
    for g in range(G):
        if g == 0:
            small[2].wait()
        ns[g] = jnp.dot(maps[g][0] + maps[g][1], nb_ref[...],
                        preferred_element_type=F32).astype(BF16)
        copy = remote(ns.at[g], stn.at[e], n1_send.at[g], n1_recv.at[e], dev(mirror, g, d))
        copy.start()
        stage1.append(copy)

    for copy in small[3:]:
        copy.wait()
    tokens = tok_ref[...].astype(F32)
    inv = lax.rsqrt(jnp.mean(tokens * tokens, axis=-1, keepdims=True) + 1e-05)
    normed = (tokens * inv * gain_ref[...]).astype(BF16)
    logits = lax.dot_general(normed, router_ref[...], (((1,), (1,)), ((), ())),
                             preferred_element_type=F32)
    lane_e = lax.broadcasted_iota(jnp.int32, logits.shape, 1).astype(F32)
    diagonal = lax.broadcasted_iota(jnp.int32, (T, T), 0) == lax.broadcasted_iota(
        jnp.int32, (T, T), 1)
    first, second = [
        jnp.sum(jnp.where(diagonal, idf_ref[k:k + 1, :].astype(F32), 0.0), axis=1, keepdims=True)
        for k in range(2)]
    l0 = jnp.sum(jnp.where(lane_e == first, logits, 0.0), axis=1, keepdims=True)
    l1 = jnp.sum(jnp.where(lane_e == second, logits, 0.0), axis=1, keepdims=True)
    lane = lax.broadcasted_iota(jnp.int32, (T, 128), 1).astype(F32)
    xall[0] = normed
    call[0] = jnp.where(lane == first, jax.nn.sigmoid(l0 - l1), 0.0) + jnp.where(
        lane == second, jax.nn.sigmoid(l1 - l0), 0.0)
    fwd = []
    for k in range(1, G):
        to = dev(p, lax.rem(e + k, G), d)
        for copy in (remote(xall.at[0], xall.at[k], x_send.at[k], x_recv.at[k], to),
                     remote(call.at[0], call.at[k], c_send.at[k], c_recv.at[k], to)):
            copy.start()
            fwd.append(copy)

    def hop(c, k, way):
        block = d - k if way == 0 else d + k
        block = jnp.clip(block, 0, Z - 1)
        to = jnp.clip(d + 1 if way == 0 else d - 1, 0, Z - 1)
        return remote(gall.at[block, c], gall.at[block, c], z_send.at[way, k, c],
                      z_recv.at[way, k, c], dev(p, e, to))

    def sends(k, way):
        return (d >= k) & (d < Z - 1) if way == 0 else (d + k < Z) & (d > 0)

    def arrives(k, way):
        return d >= k + 1 if way == 0 else d + k + 1 < Z

    def start_hops(k, c):
        for way in range(2):
            if k > 0:
                @pl.when(arrives(k - 1, way))
                def _():
                    hop(c, k - 1, way).wait_recv()

            @pl.when(sends(k, way))
            def _():
                hop(c, k, way).start()

    for c in range(CHUNKS):
        for s in range(G):
            remote(gs.at[0, c], st.at[c, s], s1_send.at[c, 0], s1_recv.at[c, s],
                   dev(mirror, 0, d)).wait_recv()
        for i in range(0, FR, TILE):
            parts = [st[c, s, i - starts[s]:i - starts[s] + TILE, :] for s in range(G)
                     if starts[s] <= i < starts[s] + W]
            gall[d, c, i:i + TILE, :] = functools.reduce(lambda a, b: a + b, parts)
        start_hops(0, c)
    for s in range(G):
        remote(ns.at[0], stn.at[s], n1_send.at[0], n1_recv.at[s], dev(mirror, 0, d)).wait_recv()
    for i in range(0, FR, TILE):
        parts = [stn[s, i - starts[s]:i - starts[s] + TILE, :] for s in range(G)
                 if starts[s] <= i < starts[s] + W]
        whole = functools.reduce(lambda a, b: a + b, parts).astype(F32)
        for z in range(Z):
            nf[z, i:i + TILE, :] = whole[:, z * DZ:(z + 1) * DZ].astype(BF16)
    spread = []
    for k in range(1, Z):
        to = lax.rem(d + k, Z)
        copy = remote(nf.at[to], nall.at[d], nz_send.at[k], nz_recv.at[k], dev(p, e, to))
        copy.start()
        spread.append(copy)
    nall[d] = nf[d]

    for copy in fwd:
        copy.wait_recv()

    def expert(j):
        for copy in weights[j]:
            copy.wait()
        block = xall[...].reshape(G * T, D)

        @pl.loop(0, BLOCKS)
        def _(c):
            cols = pl.ds(pl.multiple_of(c * (HID // BLOCKS), 128), HID // BLOCKS)
            gate = jnp.dot(block, wg[j, :, cols], preferred_element_type=F32)
            up = jnp.dot(block, wu[j, :, cols], preferred_element_type=F32)
            hid[:, cols] = (jax.nn.gelu(gate) * up).astype(BF16)

        weight = call[...].reshape(G * T, 128)
        lanes = lax.broadcasted_iota(jnp.int32, (G * T, 128), 1)
        weight = jnp.sum(jnp.where(lanes == e * L + j, weight, 0.0), axis=1, keepdims=True)

        @pl.loop(0, BLOCKS)
        def _(c):
            cols = pl.ds(pl.multiple_of(c * (D // BLOCKS), 128), D // BLOCKS)
            out = jnp.dot(hid[...], wd[j, :, cols], preferred_element_type=F32)
            out = weight * out.astype(BF16).astype(F32)
            if j == 0:
                acc[:, cols] = out
            else:
                acc[:, cols] += out

    done = 1
    for j in range(L):
        expert(j)
        if done < Z - 1:
            for c in range(CHUNKS):
                start_hops(done, c)
            done += 1

    back = []
    for k in range(1, G):
        ps[k] = acc[k * T:(k + 1) * T, :].astype(BF16)
        copy = remote(ps.at[k], rp.at[k], p_send.at[k], p_recv.at[k],
                      dev(p, lax.rem(e + G - k, G), d))
        copy.start()
        back.append(copy)
    while done < Z - 1:
        for c in range(CHUNKS):
            start_hops(done, c)
        done += 1
    total = tok_ref[...].astype(F32) + acc[0:T, :]
    for k, copy in enumerate(back):
        copy.wait_recv()
        total = total + rp[k + 1].astype(F32)
    mixed[...] = total.astype(BF16)
    onward = remote(mixed, landed, h_sem.at[0], h_sem.at[1], dev(after, e, d))
    onward.start()

    for copy in spread:
        copy.wait_recv()
    flat = nall[...].reshape(Z * FR, DZ).astype(F32)
    place = lax.rem(lax.broadcasted_iota(jnp.int32, (Z * FR, 1), 0), R)
    for j in range(L):
        mine = (place >= j * CAP) & (place < (j + 1) * CAP)
        nt[j] = jnp.where(mine, flat, 0.0).T.astype(BF16)
    for c in range(CHUNKS):
        for way in range(2):
            @pl.when(arrives(Z - 2, way))
            def _():
                hop(c, Z - 2, way).wait_recv()
        cols = slice(c * HC, (c + 1) * HC)
        for j in range(L):
            grad_ref[j, :, cols] = jnp.dot(nt[j], gall[:, c].reshape(Z * FR, HC),
                                           preferred_element_type=F32)

    onward.wait_recv()
    ho_ref[...] = landed[...]
    onward.wait_send()
    for copy in stage1 + fwd + spread + back:
        copy.wait_send()
    for k in range(Z - 1):
        for c in range(CHUNKS):
            for way in range(2):
                @pl.when(sends(k, way))
                def _():
                    hop(c, k, way).wait_send()


def shards(
    acts_fwd, ids_fwd, norm_gain, router_w, gate_w, up_w, down_w, normed_bwd, ids_bwd, dgate_bwd
):
    S, G, Z = lax.axis_size("pipe"), lax.axis_size("expert"), lax.axis_size("dp")
    L = gate_w.shape[1]
    E = G * L
    T, D = acts_fwd.shape[2:]
    HID = gate_w.shape[3]
    DZ = D // Z
    HC = HID // CHUNKS
    R = L * CAP
    FR = G * R
    W = max(-(-(s + 1) * R // TILE) * TILE - s * R // TILE * TILE for s in range(G))
    vmem = pl.BlockSpec(memory_space=pltpu.VMEM)
    hbm = pl.BlockSpec(memory_space=pltpu.HBM)
    dma = pltpu.SemaphoreType.DMA
    V = pltpu.VMEM
    handed, grad = pl.pallas_call(
        functools.partial(relay_kernel, (S, G, Z, L)),
        out_shape=(jax.ShapeDtypeStruct((T, D), BF16), jax.ShapeDtypeStruct((L, DZ, HID), F32)),
        in_specs=[hbm] * 10,
        out_specs=(vmem, vmem),
        scratch_shapes=[
            V((T, D), BF16), V((2, T), jnp.int32), V((1, D), F32), V((E, D), BF16),
            V((T, D), BF16), V((2, T), jnp.int32), V((T, 2, HID), BF16), dma((7,)),
            V((L, D, HID), BF16), V((L, D, HID), BF16), V((L, HID, D), BF16),
            V((G, CHUNKS, W, HC), BF16), V((CHUNKS, G, W, HC), BF16), V((Z, CHUNKS, FR, HC), BF16),
            V((G, W, D), BF16), V((G, W, D), BF16), V((Z, FR, DZ), BF16),
            V((Z, FR, DZ), BF16), V((L, DZ, Z * FR), BF16),
            V((G, T, D), BF16), V((G, T, 128), F32), V((G * T, HID), BF16), V((G * T, D), F32),
            V((G, T, D), BF16), V((G, T, D), BF16), V((T, D), BF16), V((T, D), BF16),
            dma((L, 3)), dma((CHUNKS, G)), dma((CHUNKS, G)), dma((G,)), dma((G,)),
            dma((2, Z - 1, CHUNKS)), dma((2, Z - 1, CHUNKS)), dma((Z,)), dma((Z,)),
            dma((G,)), dma((G,)), dma((G,)), dma((G,)), dma((G,)), dma((G,)), dma((2,)),
        ],
        compiler_params=pltpu.CompilerParams(
            collective_id=0, has_side_effects=True, vmem_limit_bytes=36 << 20),
    )(
        *[pltpu.with_memory_space_constraint(x, pltpu.HBM) for x in (acts_fwd[0, 0], ids_fwd[0, 0].T, norm_gain, router_w[0].T, gate_w[0], up_w[0], down_w[0],
        normed_bwd[0, 0], ids_bwd[0, 0].T, dgate_bwd[0, 0])]
    )
    return handed[None, None], grad[None]


def solution(mesh):
    in_specs = (
        P("pipe", "dp", "expert", None),
        P("pipe", "dp", "expert", None),
        P("pipe", None),
        P("pipe", None, None),
        P("pipe", "expert", None, None),
        P("pipe", "expert", None, None),
        P("pipe", "expert", None, None),
        P("pipe", "dp", "expert", None),
        P("pipe", "dp", "expert", None),
        P("pipe", "dp", "expert", None, None),
    )
    out_specs = (P("pipe", "dp", "expert", None), P("pipe", "expert", "dp", None))
    return jax.shard_map(shards, mesh=mesh, in_specs=in_specs, out_specs=out_specs, check_vma=False)
```

```python
import functools

import jax
import jax.numpy as jnp
from jax import lax
from jax.experimental import pallas as pl
from jax.experimental.pallas import tpu as pltpu
from jax.sharding import PartitionSpec as P

CAP = 36
TILE = 16
LANES = 128
BLOCKS = 3
CHUNKS = (1, 1, 1, 1, 2, 2, 2, 2)
F32 = jnp.float32
BF16 = jnp.bfloat16


def window_sizes(D, Z):
    DZ = D // Z
    end = -(-DZ // LANES)
    pair = max(-(-(b + 2) * DZ // LANES) - b * DZ // LANES for b in range(0, Z, 2))
    return end, pair


def message_plan(a, b):
    if not b:
        messages, at = [], 0
        for n in CHUNKS:
            messages.append((at, n, 0, a))
            at += n
        return messages, [[c] for c in range(len(CHUNKS))]
    messages, at = [(0, 1, 0, a), (1, 1, 0, a), (0, 2, a, b)], 2
    fresh = [[0], [1], []]
    for c, n in enumerate(CHUNKS):
        if c >= 2:
            messages.append((at, n, 0, a + b))
            fresh.append([c])
            at += n
    return messages, fresh


def relay_kernel(
    dims,
    tok_hbm, idf_hbm, gain_hbm, router_hbm, wg_hbm, wu_hbm, wd_hbm, nb_hbm, idb_hbm, dg_hbm,
    ho_ref, grad_ref,
    tok_ref, idf_ref, gain_ref, router_ref, nb_ref, idb_ref, dg_ref, in_sem,
    wg, wu, wd, gs, st, gall, ns, stn, nall, turned, lhs_red, lhs_own, lhs_end, ps, rp,
    xall, call, hid, acc, po, pi, mixed, landed,
    w_sem, s_send, s_recv, n_send, n_recv, nz_send, nz_recv, z_send, z_recv, r_send, r_recv,
    x_send, x_recv, c_send, c_recv, p_send, p_recv, h_sem,
):
    S, G, Z, L = dims
    T, D = tok_ref.shape
    HID = dg_ref.shape[2]
    U = HID // LANES
    DZ = D // Z
    R = L * CAP
    FR = G * R
    W = gs.shape[2]
    NTT = D // LANES
    N1, NT = window_sizes(D, Z)
    NA = min(DZ, LANES)
    NB = DZ - NA
    QS = 2 if NB else 1
    starts = [s * R // TILE * TILE for s in range(G)]
    p = lax.axis_index("pipe")
    e = lax.axis_index("expert")
    d = lax.axis_index("dp")
    mirror = S - 1 - p
    after = lax.rem(p + 1, S)
    before = lax.rem(p + S - 1, S)
    first = d == 0
    last = d == Z - 1
    is_end = first | last
    is_mid = (d > 0) & (d < Z - 1)
    is_adj = (d == 1) | (d == Z - 2)
    side = jnp.where(d < Z // 2, 0, 1)
    low = jnp.where(d == 1, 1, 0)
    end_row = pl.multiple_of(side * ((Z - 1) * DZ - LANES * (NTT - N1)), 8)
    own_row = pl.multiple_of(d * DZ - (d // 2 * 2 * DZ) // LANES * LANES, 8)
    end_dev = jnp.where(d == 1, 0, Z - 1)

    def dev(pp, ee, dd):
        return {"pipe": pp, "expert": ee, "dp": dd}

    def remote(src, dst, ss, rs, to):
        return pltpu.make_async_remote_copy(
            src_ref=src, dst_ref=dst, send_sem=ss, recv_sem=rs,
            device_id=to, device_id_type=pl.DeviceIdType.MESH)

    def local(src, dst, sem):
        return pltpu.make_async_copy(src, dst, sem)

    small = []
    for i, (src, dst) in enumerate((
        (idb_hbm, idb_ref), (dg_hbm, dg_ref), (nb_hbm, nb_ref), (tok_hbm, tok_ref),
        (idf_hbm, idf_ref), (gain_hbm, gain_ref), (router_hbm, router_ref),
    )):
        copy = local(src, dst, in_sem.at[i])
        copy.start()
        small.append(copy)

    barrier = pltpu.get_barrier_semaphore()
    peers = [dev(mirror, g, d) for g in range(G)]
    peers += [dev(p, lax.rem(e + k, G), d) for k in range(1, G)]
    peers += [dev(p, e, lax.rem(d + k, Z)) for k in range(1, Z)]
    peers += [dev(after, e, d), dev(before, e, d)]
    for peer in peers:
        pl.semaphore_signal(barrier, inc=1, device_id=peer, device_id_type=pl.DeviceIdType.MESH)

    weights = []
    for j in range(L):
        trio = [local(wg_hbm.at[j], wg.at[j], w_sem.at[j, 0]),
                local(wu_hbm.at[j], wu.at[j], w_sem.at[j, 1]),
                local(wd_hbm.at[j], wd.at[j], w_sem.at[j, 2])]
        for copy in trio:
            copy.start()
        weights.append(trio)

    small[0].wait()
    ids = [idb_ref[k:k + 1, :].astype(F32) for k in range(2)]
    labels = lax.broadcasted_iota(jnp.int32, (8, T), 0).astype(F32)
    onehot = [jnp.where(ids[k] == labels, 1.0, 0.0) for k in range(2)]
    earlier = lax.broadcasted_iota(jnp.int32, (T, T), 0) < lax.broadcasted_iota(
        jnp.int32, (T, T), 1)
    earlier = jnp.where(earlier, 1.0, 0.0).astype(BF16)
    counts = [jnp.dot(onehot[k].astype(BF16), earlier, preferred_element_type=F32)
              for k in range(2)]
    counts[1] = counts[1] + jnp.sum(onehot[0], axis=1, keepdims=True)
    rank = [jnp.sum(counts[k] * onehot[k], axis=0, keepdims=True) for k in range(2)]
    shift = lax.rem(e * R, TILE).astype(F32)
    slots = lax.broadcasted_iota(jnp.int32, (W, T), 0).astype(F32)
    maps = []
    for g in range(G):
        pair = []
        for k in range(2):
            own = jnp.where((ids[k] >= g * L) & (ids[k] < (g + 1) * L),
                            shift + (ids[k] - g * L) * CAP + rank[k], -1.0)
            pair.append(jnp.where(slots == own, 1.0, 0.0).astype(BF16))
        maps.append(pair)
    both = jnp.concatenate([jnp.concatenate(pair, axis=1) for pair in maps], axis=0)

    spans = []
    at = 0
    for n in CHUNKS:
        spans.append((at, n))
        at += n
    assert at == U
    messages, fresh = message_plan(L * NA, L * NB)

    def units(ref, c):
        return ref.at[pl.ds(spans[c][0], spans[c][1])]

    def stage(c, g):
        return remote(units(gs.at[g], c), units(st.at[e], c), s_send.at[c, g], s_recv.at[c, e],
                      dev(mirror, g, d))

    def route(c):
        u, n = spans[c]
        cols = slice(u * LANES, (u + n) * LANES)
        picked = jnp.concatenate([dg_ref[:, 0, cols], dg_ref[:, 1, cols]], axis=0)
        placed = jnp.dot(both, picked, preferred_element_type=F32).astype(BF16)
        for g in range(G):
            for i in range(n):
                gs[g, u + i] = placed[g * W:(g + 1) * W, i * LANES:(i + 1) * LANES]

    def send_stage(c):
        for g in range(G):
            stage(c, g).start()

    bounds = [0, 2, 2 * N1, NTT] if QS > 1 else [0, 2, NTT]
    Q = len(bounds) - 1

    def rows_stage(q, g):
        span = pl.ds(bounds[q], bounds[q + 1] - bounds[q])
        return remote(ns.at[g, span], stn.at[e, span], n_send.at[q, g], n_recv.at[q, e],
                      dev(mirror, g, d))

    def send_rows(q):
        for g in range(G):
            rows_stage(q, g).start()

    def window(b):
        lo = b // 2 * 2 * DZ // LANES
        return range(lo, min(lo + NT, NTT))

    def place_of(t):
        return 2 * t if t < NTT // 2 else 2 * (NTT - 1 - t) + 1

    def rows_gather(i, r, to):
        return remote(nall.at[r, i], nall.at[r, i], nz_send.at[i, to], nz_recv.at[i, r],
                      dev(p, e, to))

    def rows_dests(i):
        return [b for b in range(1, Z - 1) if i in [place_of(t) for t in window(b)]]

    def combine_rows(q):
        for s in range(G):
            span = pl.ds(bounds[q], bounds[q + 1] - bounds[q])
            remote(ns.at[0, span], stn.at[s, span], n_send.at[q, 0], n_recv.at[q, s],
                   dev(mirror, 0, d)).wait_recv()
        for i in range(bounds[q], bounds[q + 1]):
            for row in range(0, FR, TILE):
                parts = [stn[s, i, row - starts[s]:row - starts[s] + TILE, :] for s in range(G)
                         if starts[s] <= row < starts[s] + W]
                nall[d, i, row:row + TILE, :] = functools.reduce(lambda a, b: a + b, parts)
            for to in rows_dests(i):
                @pl.when(d != to)
                def _():
                    rows_gather(i, d, to).start()

    def rows_arrive(i, r):
        rows_gather(i, r, 1).wait_recv()

    def wait_rows_sent():
        for q in range(Q):
            for g in range(G):
                rows_stage(q, g).wait_send()
        for i in range(NTT):
            for to in rows_dests(i):
                @pl.when(d != to)
                def _():
                    rows_gather(i, d, to).wait_send()

    def gather(c, r, to):
        return remote(units(gall.at[r], c), units(gall.at[r], c), z_send.at[c, to],
                      z_recv.at[c, r], dev(p, e, to))

    def combine(c):
        for s in range(G):
            remote(units(gs.at[0], c), units(st.at[s], c), s_send.at[c, 0], s_recv.at[c, s],
                   dev(mirror, 0, d)).wait_recv()
        u, n = spans[c]
        for v in range(u, u + n):
            for i in range(0, FR, TILE):
                parts = [st[s, v, i - starts[s]:i - starts[s] + TILE, :] for s in range(G)
                         if starts[s] <= i < starts[s] + W]
                gall[d, v, i:i + TILE, :] = functools.reduce(lambda a, b: a + b, parts)
        order = [Z - 2, 1] + list(range(2, Z - 2))
        for to in order:
            @pl.when((d != to) & first)
            def _():
                gather(c, d, to).start()
        order[0:2] = [1, Z - 2]
        for to in order:
            @pl.when((d != to) & (d > 0))
            def _():
                gather(c, d, to).start()

    def mask_into(lhs, at, row, n, height):
        whole = turned[pl.ds(pl.multiple_of(row, 8), n), 0:height]
        place = lax.rem(lax.broadcasted_iota(jnp.int32, (1, height), 1), R)
        for j in range(L):
            mine = (place >= j * CAP) & (place < (j + 1) * CAP)
            lhs[at + j * n:at + (j + 1) * n, :] = jnp.where(mine, whole, 0.0).astype(BF16)

    def turn(t, block):
        turned[t * LANES:(t + 1) * LANES, 0:block.shape[0]] = block.astype(F32).T

    def rows_for_end(q):
        at, n = [(0, NA), (L * NA, NB)][q]
        i = 2 * q + side

        @pl.when(is_adj)
        def _():
            for k in range(Z - 1):
                @pl.when(low + k != d)
                def _():
                    rows_arrive(i, low + k)
            turn(0, nall[pl.ds(low, Z - 1), i].reshape((Z - 1) * FR, LANES))
            mask_into(lhs_red, at, side * (LANES - n), n, (Z - 1) * FR)

    def rows_for_own():
        for b in range(1, Z - 1):
            @pl.when(d == b)
            def _():
                for t in window(b):
                    i = place_of(t)
                    early = b in (1, Z - 2) and i in range(int(b != 1), 2 * QS, 2)
                    for r in range(Z):
                        if r != b and not (early and r != (0 if b == 1 else Z - 1)):
                            rows_arrive(i, r)
                for k, t in enumerate(window(b)):
                    turn(k, nall[:, place_of(t)].reshape(Z * FR, LANES))
                mask_into(lhs_own, 0, own_row, DZ, Z * FR)
        for b in (0, Z - 1):
            @pl.when(d == b)
            def _():
                for k in range(N1):
                    t = k if b == 0 else NTT - N1 + k
                    turn(k, nall[b, place_of(t)])
                mask_into(lhs_end, 0, end_row, DZ, FR)

    def block_arrives(c, r):
        return gather(c, r, 1)

    def onto_end(m):
        u, n, lo, h = messages[m]
        at = (pl.ds(u, n), pl.ds(lo, h))
        return remote(ps.at[at], rp.at[at], r_send.at[m], r_recv.at[m], dev(p, e, end_dev))

    def reduce(m):
        u, n, lo, h = messages[m]

        @pl.when(is_adj)
        def _():
            for c in fresh[m]:
                for i in range(Z - 1):
                    @pl.when(low + i != d)
                    def _():
                        block_arrives(c, low + i).wait_recv()
            block = jnp.concatenate(
                [gall[pl.ds(low, Z - 1), u + i].reshape((Z - 1) * FR, LANES) for i in range(n)],
                axis=1)
            part = jnp.dot(lhs_red[lo:lo + h, :], block, preferred_element_type=F32).astype(BF16)
            for i in range(n):
                ps[u + i, lo:lo + h, :] = part[:, i * LANES:(i + 1) * LANES]
            onto_end(m).start()

    def own_wait(c):
        @pl.when(is_adj)
        def _():
            block_arrives(c, jnp.where(d == 1, 0, Z - 1)).wait_recv()
        if Z > 4:
            @pl.when(is_mid & jnp.logical_not(is_adj))
            def _():
                for r in range(Z):
                    @pl.when(d != r)
                    def _():
                        block_arrives(c, r).wait_recv()

    def own_term(u, n):
        cols = slice(u * LANES, (u + n) * LANES)

        @pl.when(is_mid)
        def _():
            block = jnp.concatenate(
                [gall[:, u + i].reshape(Z * FR, LANES) for i in range(n)], axis=1)
            whole = jnp.dot(lhs_own[...], block, preferred_element_type=F32)
            for j in range(L):
                grad_ref[j, :, cols] = whole[j * DZ:(j + 1) * DZ]

        @pl.when(is_end)
        def _():
            block = jnp.concatenate([gall[d, u + i] for i in range(n)], axis=1)
            whole = jnp.dot(lhs_end[...], block, preferred_element_type=F32)
            for j in range(L):
                grad_ref[j, :, cols] = whole[j * DZ:(j + 1) * DZ]

    def add_part(m):
        u, n, lo, h = messages[m]

        @pl.when(is_end)
        def _():
            onto_end(m).wait_recv()
            for i in range(u, u + n):
                cols = slice(i * LANES, (i + 1) * LANES)
                for at, size, row in ((0, NA, side * NB), (L * NA, NB, (1 - side) * NA)):
                    if size and lo <= at < lo + h:
                        for j in range(L):
                            rows_of = pl.ds(pl.multiple_of(row, 8), size)
                            grad_ref[j, rows_of, cols] += rp[
                                i, at + j * size:at + (j + 1) * size].astype(F32)

    def forward_tokens():
        for copy in small[3:]:
            copy.wait()
        tokens = tok_ref[...].astype(F32)
        inv = lax.rsqrt(jnp.mean(tokens * tokens, axis=-1, keepdims=True) + 1e-05)
        normed = (tokens * inv * gain_ref[...]).astype(BF16)
        logits = lax.dot_general(normed, router_ref[...], (((1,), (1,)), ((), ())),
                                 preferred_element_type=F32)
        lane_e = lax.broadcasted_iota(jnp.int32, logits.shape, 1).astype(F32)
        diagonal = lax.broadcasted_iota(jnp.int32, (T, T), 0) == lax.broadcasted_iota(
            jnp.int32, (T, T), 1)
        one, two = [
            jnp.sum(jnp.where(diagonal, idf_ref[k:k + 1, :].astype(F32), 0.0), axis=1,
                    keepdims=True)
            for k in range(2)]
        l0 = jnp.sum(jnp.where(lane_e == one, logits, 0.0), axis=1, keepdims=True)
        l1 = jnp.sum(jnp.where(lane_e == two, logits, 0.0), axis=1, keepdims=True)
        lane = lax.broadcasted_iota(jnp.int32, (T, LANES), 1).astype(F32)
        xall[0] = normed
        call[0] = jnp.where(lane == one, jax.nn.sigmoid(l0 - l1), 0.0) + jnp.where(
            lane == two, jax.nn.sigmoid(l1 - l0), 0.0)
        for copy in tokens_out:
            copy.start()

    tokens_out = []
    for k in range(1, G):
        to = dev(p, lax.rem(e + k, G), d)
        tokens_out += [remote(xall.at[0], xall.at[k], x_send.at[k], x_recv.at[k], to),
                       remote(call.at[0], call.at[k], c_send.at[k], c_recv.at[k], to)]

    def tokens_in():
        for copy in tokens_out:
            copy.wait_recv()

    def widen(j, c):
        if c == 0:
            weights[j][0].wait()
            weights[j][1].wait()
        n = HID // BLOCKS
        cols = slice(c * n, (c + 1) * n)
        block = xall[...].reshape(G * T, D)
        gate = jnp.dot(block, wg[j, :, cols], preferred_element_type=F32)
        up = jnp.dot(block, wu[j, :, cols], preferred_element_type=F32)
        hid[:, cols] = (jax.nn.gelu(gate) * up).astype(BF16)

    def narrow(j):
        weights[j][2].wait()
        weight = call[...].reshape(G * T, LANES)
        lanes = lax.broadcasted_iota(jnp.int32, (G * T, LANES), 1)
        weight = jnp.sum(jnp.where(lanes == e * L + j, weight, 0.0), axis=1, keepdims=True)
        for c in range(BLOCKS):
            cols = slice(c * (D // BLOCKS), (c + 1) * (D // BLOCKS))
            out = jnp.dot(hid[...], wd[j, :, cols], preferred_element_type=F32)
            out = weight * out.astype(BF16).astype(F32)
            if j == 0:
                acc[:, cols] = out
            else:
                acc[:, cols] += out

    back = []
    for k in range(1, G):
        back.append(remote(po.at[k], pi.at[k], p_send.at[k], p_recv.at[k],
                           dev(p, lax.rem(e + G - k, G), d)))
    onward = remote(mixed, landed, h_sem.at[0], h_sem.at[1], dev(after, e, d))

    def give_back():
        for k in range(1, G):
            po[k] = acc[k * T:(k + 1) * T, :].astype(BF16)
            back[k - 1].start()

    def hand_on():
        total = tok_ref[...].astype(F32) + acc[0:T, :]
        for k, copy in enumerate(back):
            copy.wait_recv()
            total = total + pi[k + 1].astype(F32)
        mixed[...] = total.astype(BF16)
        onward.start()

    C = len(spans)

    def sent(c):
        for g in range(G):
            stage(c, g).wait_send()
        for to in range(1, Z - 1):
            @pl.when(d != to)
            def _():
                gather(c, d, to).wait_send()

    def parts_sent():
        @pl.when(is_adj)
        def _():
            for m in range(len(messages)):
                onto_end(m).wait_send()

    def route_rows():
        small[2].wait()
        for g in range(G):
            placed = jnp.dot(maps[g][0] + maps[g][1], nb_ref[...],
                             preferred_element_type=F32).astype(BF16)
            for t in range(NTT):
                ns[g, place_of(t)] = placed[:, t * LANES:(t + 1) * LANES]

    def out(c):
        route(c)
        send_stage(c)

    M = len(messages)
    extra = M - C

    small[1].wait()
    route(0)
    pl.semaphore_wait(barrier, len(peers))
    send_stage(0)
    route_rows()
    send_rows(0)
    out(1)
    out(2)
    if QS > 1:
        send_rows(1)
    out(3)
    out(4)
    out(5)
    combine(0)
    combine_rows(0)
    out(6)
    out(7)
    send_rows(Q - 1)
    forward_tokens()
    combine(1)
    combine(2)
    rows_for_end(0)
    reduce(0)
    if QS > 1:
        combine_rows(1)
    combine(3)
    reduce(1)
    if QS > 1:
        rows_for_end(1)
        reduce(2)
    combine(4)
    reduce(2 + extra)
    tokens_in()
    widen(0, 0)
    combine(5)
    reduce(3 + extra)
    widen(0, 1)
    widen(0, 2)
    combine(6)
    reduce(4 + extra)
    narrow(0)
    if L > 1:
        widen(1, 0)
    combine(7)
    reduce(5 + extra)
    if L > 1:
        widen(1, 1)
        widen(1, 2)
    reduce(6 + extra)
    if L > 1:
        narrow(1)
    give_back()
    combine_rows(Q - 1)
    rows_for_own()
    reduce(7 + extra)
    hand_on()
    for c in range(C):
        own_wait(c)
    for u in range(0, U, 2):
        own_term(u, 2)
    for c in range(C):
        sent(c)
    wait_rows_sent()
    for copy in tokens_out + back:
        copy.wait_send()
    onward.wait_recv()
    ho_ref[...] = landed[...]
    onward.wait_send()
    for m in range(M):
        add_part(m)
    parts_sent()


def shards(
    acts_fwd, ids_fwd, norm_gain, router_w, gate_w, up_w, down_w, normed_bwd, ids_bwd, dgate_bwd
):
    S, G, Z = lax.axis_size("pipe"), lax.axis_size("expert"), lax.axis_size("dp")
    L = gate_w.shape[1]
    E = G * L
    T, D = acts_fwd.shape[2:]
    HID = gate_w.shape[3]
    U = HID // LANES
    C = len(CHUNKS)
    DZ = D // Z
    R = L * CAP
    FR = G * R
    W = max(-(-(s + 1) * R // TILE) * TILE - s * R // TILE * TILE for s in range(G))
    NTT = D // LANES
    N1, NT = window_sizes(D, Z)
    M = len(message_plan(L * min(DZ, LANES), L * (DZ - min(DZ, LANES)))[0])
    vmem = pl.BlockSpec(memory_space=pltpu.VMEM)
    hbm = pl.BlockSpec(memory_space=pltpu.HBM)
    dma = pltpu.SemaphoreType.DMA
    V = pltpu.VMEM
    handed, grad = pl.pallas_call(
        functools.partial(relay_kernel, (S, G, Z, L)),
        out_shape=(jax.ShapeDtypeStruct((T, D), BF16), jax.ShapeDtypeStruct((L, DZ, HID), F32)),
        in_specs=[hbm] * 10,
        out_specs=(vmem, vmem),
        scratch_shapes=[
            V((T, D), BF16), V((2, T), jnp.int32), V((1, D), F32), V((E, D), BF16),
            V((T, D), BF16), V((2, T), jnp.int32), V((T, 2, HID), BF16), dma((7,)),
            V((L, D, HID), BF16), V((L, D, HID), BF16), V((L, HID, D), BF16),
            V((G, U, W, LANES), BF16), V((G, U, W, LANES), BF16), V((Z, U, FR, LANES), BF16),
            V((G, NTT, W, LANES), BF16), V((G, NTT, W, LANES), BF16),
            V((Z, NTT, FR, LANES), BF16), V((NT * LANES, Z * FR), F32),
            V((L * DZ, (Z - 1) * FR), BF16), V((L * DZ, Z * FR), BF16), V((L * DZ, FR), BF16),
            V((U, L * DZ, LANES), BF16), V((U, L * DZ, LANES), BF16),
            V((G, T, D), BF16), V((G, T, LANES), F32), V((G * T, HID), BF16), V((G * T, D), F32),
            V((G, T, D), BF16), V((G, T, D), BF16), V((T, D), BF16), V((T, D), BF16),
            dma((L, 3)), dma((C, G)), dma((C, G)), dma((3, G)), dma((3, G)), dma((NTT, Z)), dma((NTT, Z)),
            dma((C, Z)), dma((C, Z)), dma((M,)), dma((M,)),
            dma((G,)), dma((G,)), dma((G,)), dma((G,)), dma((G,)), dma((G,)), dma((2,)),
        ],
        compiler_params=pltpu.CompilerParams(
            collective_id=0, has_side_effects=True, vmem_limit_bytes=36 << 20),
    )(*(pltpu.with_memory_space_constraint(x, pltpu.HBM) for x in (
        acts_fwd[0, 0], ids_fwd[0, 0].T, norm_gain, router_w[0].T, gate_w[0], up_w[0], down_w[0],
        normed_bwd[0, 0], ids_bwd[0, 0].T, dgate_bwd[0, 0],
    )))
    return handed[None, None], grad[None]


def solution(mesh):
    in_specs = (
        P("pipe", "dp", "expert", None),
        P("pipe", "dp", "expert", None),
        P("pipe", None),
        P("pipe", None, None),
        P("pipe", "expert", None, None),
        P("pipe", "expert", None, None),
        P("pipe", "expert", None, None),
        P("pipe", "dp", "expert", None),
        P("pipe", "dp", "expert", None),
        P("pipe", "dp", "expert", None, None),
    )
    out_specs = (P("pipe", "dp", "expert", None), P("pipe", "expert", "dp", None))
    return jax.shard_map(shards, mesh=mesh, in_specs=in_specs, out_specs=out_specs, check_vma=False)
```

```python
import functools

import jax
import jax.numpy as jnp
from jax import lax
from jax.experimental import pallas as pl
from jax.experimental.pallas import tpu as pltpu
from jax.sharding import PartitionSpec as P

CAP = 36
TILE = 16
LANES = 128
BLOCKS = 3
CHUNKS = (1, 1, 1, 1, 2, 2, 2, 2)
F32 = jnp.float32
BF16 = jnp.bfloat16


def window_sizes(D, Z):
    DZ = D // Z
    end = -(-DZ // LANES)
    pair = max(-(-(b + 2) * DZ // LANES) - b * DZ // LANES for b in range(0, Z, 2))
    return end, pair


def message_plan(a, b):
    if not b:
        messages, at = [], 0
        for n in CHUNKS:
            messages.append((at, n, 0, a))
            at += n
        return messages, [[c] for c in range(len(CHUNKS))]
    messages, at = [(0, 1, 0, a), (1, 1, 0, a), (0, 2, a, b)], 2
    fresh = [[0], [1], []]
    for c, n in enumerate(CHUNKS):
        if c >= 2:
            messages.append((at, n, 0, a + b))
            fresh.append([c])
            at += n
    return messages, fresh


def relay_kernel(
    dims,
    tok_hbm, idf_hbm, gain_hbm, router_hbm, wg_hbm, wu_hbm, wd_hbm, nb_hbm, idb_hbm, dg_hbm,
    ho_ref, grad_ref,
    tok_ref, idf_ref, gain_ref, router_ref, nb_ref, idb_ref, dg_ref, in_sem,
    wg, wu, wd, gs, st, gall, ns, stn, nall, turned, lhs_red, lhs_own, lhs_end, ps, rp,
    xall, call, hid, acc, po, pi, mixed, landed,
    w_sem, s_send, s_recv, n_send, n_recv, nz_send, nz_recv, z_send, z_recv, r_send, r_recv,
    x_send, x_recv, c_send, c_recv, p_send, p_recv, h_sem,
):
    S, G, Z, L = dims
    T, D = tok_ref.shape
    HID = dg_ref.shape[2]
    U = HID // LANES
    DZ = D // Z
    R = L * CAP
    FR = G * R
    W = gs.shape[2]
    NTT = D // LANES
    N1, NT = window_sizes(D, Z)
    NA = min(DZ, LANES)
    NB = DZ - NA
    QS = 2 if NB else 1
    starts = [s * R // TILE * TILE for s in range(G)]
    p = lax.axis_index("pipe")
    e = lax.axis_index("expert")
    d = lax.axis_index("dp")
    mirror = S - 1 - p
    after = lax.rem(p + 1, S)
    before = lax.rem(p + S - 1, S)
    first = d == 0
    last = d == Z - 1
    is_end = first | last
    is_mid = (d > 0) & (d < Z - 1)
    is_adj = (d == 1) | (d == Z - 2)
    side = jnp.where(d < Z // 2, 0, 1)
    low = jnp.where(d == 1, 1, 0)
    end_row = pl.multiple_of(side * ((Z - 1) * DZ - LANES * (NTT - N1)), 8)
    own_row = pl.multiple_of(d * DZ - (d // 2 * 2 * DZ) // LANES * LANES, 8)
    end_dev = jnp.where(d == 1, 0, Z - 1)

    def dev(pp, ee, dd):
        return {"pipe": pp, "expert": ee, "dp": dd}

    def remote(src, dst, ss, rs, to):
        return pltpu.make_async_remote_copy(
            src_ref=src, dst_ref=dst, send_sem=ss, recv_sem=rs,
            device_id=to, device_id_type=pl.DeviceIdType.MESH)

    def local(src, dst, sem):
        return pltpu.make_async_copy(src, dst, sem)

    small = []
    for i, (src, dst) in enumerate((
        (idb_hbm, idb_ref), (dg_hbm, dg_ref), (nb_hbm, nb_ref), (tok_hbm, tok_ref),
        (idf_hbm, idf_ref), (gain_hbm, gain_ref), (router_hbm, router_ref),
    )):
        copy = local(src, dst, in_sem.at[i])
        copy.start()
        small.append(copy)

    barrier = pltpu.get_barrier_semaphore()
    peers = [dev(mirror, g, d) for g in range(G)]
    peers += [dev(p, lax.rem(e + k, G), d) for k in range(1, G)]
    peers += [dev(p, e, lax.rem(d + k, Z)) for k in range(1, Z)]
    peers += [dev(after, e, d), dev(before, e, d)]
    for peer in peers:
        pl.semaphore_signal(barrier, inc=1, device_id=peer, device_id_type=pl.DeviceIdType.MESH)

    weights = []
    for j in range(L):
        trio = [local(wg_hbm.at[j], wg.at[j], w_sem.at[j, 0]),
                local(wu_hbm.at[j], wu.at[j], w_sem.at[j, 1]),
                local(wd_hbm.at[j], wd.at[j], w_sem.at[j, 2])]
        for copy in trio:
            copy.start()
        weights.append(trio)

    small[0].wait()
    ids = [idb_ref[k:k + 1, :].astype(F32) for k in range(2)]
    labels = lax.broadcasted_iota(jnp.int32, (8, T), 0).astype(F32)
    onehot = [jnp.where(ids[k] == labels, 1.0, 0.0) for k in range(2)]
    earlier = lax.broadcasted_iota(jnp.int32, (T, T), 0) < lax.broadcasted_iota(
        jnp.int32, (T, T), 1)
    earlier = jnp.where(earlier, 1.0, 0.0).astype(BF16)
    counts = [jnp.dot(onehot[k].astype(BF16), earlier, preferred_element_type=F32)
              for k in range(2)]
    counts[1] = counts[1] + jnp.sum(onehot[0], axis=1, keepdims=True)
    rank = [jnp.sum(counts[k] * onehot[k], axis=0, keepdims=True) for k in range(2)]
    shift = lax.rem(e * R, TILE).astype(F32)
    slots = lax.broadcasted_iota(jnp.int32, (W, T), 0).astype(F32)
    maps = []
    for g in range(G):
        pair = []
        for k in range(2):
            own = jnp.where((ids[k] >= g * L) & (ids[k] < (g + 1) * L),
                            shift + (ids[k] - g * L) * CAP + rank[k], -1.0)
            pair.append(jnp.where(slots == own, 1.0, 0.0).astype(BF16))
        maps.append(pair)
    both = jnp.concatenate([jnp.concatenate(pair, axis=1) for pair in maps], axis=0)

    spans = []
    at = 0
    for n in CHUNKS:
        spans.append((at, n))
        at += n
    assert at == U
    messages, fresh = message_plan(L * NA, L * NB)

    def units(ref, c):
        return ref.at[pl.ds(spans[c][0], spans[c][1])]

    def stage(c, g):
        return remote(units(gs.at[g], c), units(st.at[e], c), s_send.at[c, g], s_recv.at[c, e],
                      dev(mirror, g, d))

    def route(c):
        u, n = spans[c]
        cols = slice(u * LANES, (u + n) * LANES)
        picked = jnp.concatenate([dg_ref[:, 0, cols], dg_ref[:, 1, cols]], axis=0)
        placed = jnp.dot(both, picked, preferred_element_type=F32).astype(BF16)
        for g in range(G):
            for i in range(n):
                gs[g, u + i] = placed[g * W:(g + 1) * W, i * LANES:(i + 1) * LANES]

    def send_stage(c):
        for g in range(G):
            stage(c, g).start()

    bounds = [0, 2, 2 * N1, NTT] if QS > 1 else [0, 2, NTT]
    Q = len(bounds) - 1

    def rows_stage(q, g):
        span = pl.ds(bounds[q], bounds[q + 1] - bounds[q])
        return remote(ns.at[g, span], stn.at[e, span], n_send.at[q, g], n_recv.at[q, e],
                      dev(mirror, g, d))

    def send_rows(q):
        for g in range(G):
            rows_stage(q, g).start()

    def window(b):
        lo = b // 2 * 2 * DZ // LANES
        return range(lo, min(lo + NT, NTT))

    def place_of(t):
        return 2 * t if t < NTT // 2 else 2 * (NTT - 1 - t) + 1

    def rows_gather(i, r, to):
        return remote(nall.at[r, i], nall.at[r, i], nz_send.at[i, to], nz_recv.at[i, r],
                      dev(p, e, to))

    def rows_dests(i):
        return [b for b in range(1, Z - 1) if i in [place_of(t) for t in window(b)]]

    def combine_rows(q):
        for s in range(G):
            span = pl.ds(bounds[q], bounds[q + 1] - bounds[q])
            remote(ns.at[0, span], stn.at[s, span], n_send.at[q, 0], n_recv.at[q, s],
                   dev(mirror, 0, d)).wait_recv()
        for i in range(bounds[q], bounds[q + 1]):
            for row in range(0, FR, TILE):
                parts = [stn[s, i, row - starts[s]:row - starts[s] + TILE, :] for s in range(G)
                         if starts[s] <= row < starts[s] + W]
                nall[d, i, row:row + TILE, :] = functools.reduce(lambda a, b: a + b, parts)
            for to in rows_dests(i):
                @pl.when(d != to)
                def _():
                    rows_gather(i, d, to).start()

    def rows_arrive(i, r):
        rows_gather(i, r, 1).wait_recv()

    def wait_rows_sent():
        for q in range(Q):
            for g in range(G):
                rows_stage(q, g).wait_send()
        for i in range(NTT):
            for to in rows_dests(i):
                @pl.when(d != to)
                def _():
                    rows_gather(i, d, to).wait_send()

    def gather(c, r, to):
        return remote(units(gall.at[r], c), units(gall.at[r], c), z_send.at[c, to],
                      z_recv.at[c, r], dev(p, e, to))

    def combine(c):
        for s in range(G):
            remote(units(gs.at[0], c), units(st.at[s], c), s_send.at[c, 0], s_recv.at[c, s],
                   dev(mirror, 0, d)).wait_recv()
        u, n = spans[c]
        for v in range(u, u + n):
            for i in range(0, FR, TILE):
                parts = [st[s, v, i - starts[s]:i - starts[s] + TILE, :] for s in range(G)
                         if starts[s] <= i < starts[s] + W]
                gall[d, v, i:i + TILE, :] = functools.reduce(lambda a, b: a + b, parts)
        order = [Z - 2, 1] + list(range(2, Z - 2))
        for to in order:
            @pl.when((d != to) & first)
            def _():
                gather(c, d, to).start()
        order[0:2] = [1, Z - 2]
        for to in order:
            @pl.when((d != to) & (d > 0))
            def _():
                gather(c, d, to).start()

    def mask_into(lhs, at, row, n, height):
        whole = turned[pl.ds(pl.multiple_of(row, 8), n), 0:height]
        place = lax.rem(lax.broadcasted_iota(jnp.int32, (1, height), 1), R)
        for j in range(L):
            mine = (place >= j * CAP) & (place < (j + 1) * CAP)
            lhs[at + j * n:at + (j + 1) * n, :] = jnp.where(mine, whole, 0.0).astype(BF16)

    def turn(t, block):
        turned[t * LANES:(t + 1) * LANES, 0:block.shape[0]] = block.astype(F32).T

    def rows_for_end(q):
        at, n = [(0, NA), (L * NA, NB)][q]
        i = 2 * q + side

        @pl.when(is_adj)
        def _():
            for k in range(Z - 1):
                @pl.when(low + k != d)
                def _():
                    rows_arrive(i, low + k)
            turn(0, nall[pl.ds(low, Z - 1), i].reshape((Z - 1) * FR, LANES))
            mask_into(lhs_red, at, side * (LANES - n), n, (Z - 1) * FR)

    def rows_for_own():
        for b in range(1, Z - 1):
            @pl.when(d == b)
            def _():
                for t in window(b):
                    i = place_of(t)
                    early = b in (1, Z - 2) and i in range(int(b != 1), 2 * QS, 2)
                    for r in range(Z):
                        if r != b and not (early and r != (0 if b == 1 else Z - 1)):
                            rows_arrive(i, r)
                for k, t in enumerate(window(b)):
                    turn(k, nall[:, place_of(t)].reshape(Z * FR, LANES))
                mask_into(lhs_own, 0, own_row, DZ, Z * FR)
        for b in (0, Z - 1):
            @pl.when(d == b)
            def _():
                for k in range(N1):
                    t = k if b == 0 else NTT - N1 + k
                    turn(k, nall[b, place_of(t)])
                mask_into(lhs_end, 0, end_row, DZ, FR)

    def block_arrives(c, r):
        return gather(c, r, 1)

    def onto_end(m):
        u, n, lo, h = messages[m]
        at = (pl.ds(u, n), pl.ds(lo, h))
        return remote(ps.at[at], rp.at[at], r_send.at[m], r_recv.at[m], dev(p, e, end_dev))

    def reduce(m):
        u, n, lo, h = messages[m]

        @pl.when(is_adj)
        def _():
            for c in fresh[m]:
                for i in range(Z - 1):
                    @pl.when(low + i != d)
                    def _():
                        block_arrives(c, low + i).wait_recv()
            block = jnp.concatenate(
                [gall[pl.ds(low, Z - 1), u + i].reshape((Z - 1) * FR, LANES) for i in range(n)],
                axis=1)
            part = jnp.dot(lhs_red[lo:lo + h, :], block, preferred_element_type=F32).astype(BF16)
            for i in range(n):
                ps[u + i, lo:lo + h, :] = part[:, i * LANES:(i + 1) * LANES]
            onto_end(m).start()

    def own_wait(c):
        @pl.when(is_adj)
        def _():
            block_arrives(c, jnp.where(d == 1, 0, Z - 1)).wait_recv()
        if Z > 4:
            @pl.when(is_mid & jnp.logical_not(is_adj))
            def _():
                for r in range(Z):
                    @pl.when(d != r)
                    def _():
                        block_arrives(c, r).wait_recv()

    def own_term(u, n):
        cols = slice(u * LANES, (u + n) * LANES)

        @pl.when(is_mid)
        def _():
            block = jnp.concatenate(
                [gall[:, u + i].reshape(Z * FR, LANES) for i in range(n)], axis=1)
            whole = jnp.dot(lhs_own[...], block, preferred_element_type=F32)
            for j in range(L):
                grad_ref[j, :, cols] = whole[j * DZ:(j + 1) * DZ]

        @pl.when(is_end)
        def _():
            block = jnp.concatenate([gall[d, u + i] for i in range(n)], axis=1)
            whole = jnp.dot(lhs_end[...], block, preferred_element_type=F32)
            for j in range(L):
                grad_ref[j, :, cols] = whole[j * DZ:(j + 1) * DZ]

    def add_part(m):
        u, n, lo, h = messages[m]

        @pl.when(is_end)
        def _():
            onto_end(m).wait_recv()
            for i in range(u, u + n):
                cols = slice(i * LANES, (i + 1) * LANES)
                for at, size, row in ((0, NA, side * NB), (L * NA, NB, (1 - side) * NA)):
                    if size and lo <= at < lo + h:
                        for j in range(L):
                            rows_of = pl.ds(pl.multiple_of(row, 8), size)
                            grad_ref[j, rows_of, cols] += rp[
                                i, at + j * size:at + (j + 1) * size].astype(F32)

    def forward_tokens():
        for copy in small[3:]:
            copy.wait()
        tokens = tok_ref[...].astype(F32)
        inv = lax.rsqrt(jnp.mean(tokens * tokens, axis=-1, keepdims=True) + 1e-05)
        normed = (tokens * inv * gain_ref[...]).astype(BF16)
        logits = lax.dot_general(normed, router_ref[...], (((1,), (1,)), ((), ())),
                                 preferred_element_type=F32)
        lane_e = lax.broadcasted_iota(jnp.int32, logits.shape, 1).astype(F32)
        diagonal = lax.broadcasted_iota(jnp.int32, (T, T), 0) == lax.broadcasted_iota(
            jnp.int32, (T, T), 1)
        one, two = [
            jnp.sum(jnp.where(diagonal, idf_ref[k:k + 1, :].astype(F32), 0.0), axis=1,
                    keepdims=True)
            for k in range(2)]
        l0 = jnp.sum(jnp.where(lane_e == one, logits, 0.0), axis=1, keepdims=True)
        l1 = jnp.sum(jnp.where(lane_e == two, logits, 0.0), axis=1, keepdims=True)
        lane = lax.broadcasted_iota(jnp.int32, (T, LANES), 1).astype(F32)
        xall[0] = normed
        call[0] = jnp.where(lane == one, jax.nn.sigmoid(l0 - l1), 0.0) + jnp.where(
            lane == two, jax.nn.sigmoid(l1 - l0), 0.0)
        for copy in tokens_out:
            copy.start()

    tokens_out = []
    for k in range(1, G):
        to = dev(p, lax.rem(e + k, G), d)
        tokens_out += [remote(xall.at[0], xall.at[k], x_send.at[k], x_recv.at[k], to),
                       remote(call.at[0], call.at[k], c_send.at[k], c_recv.at[k], to)]

    def tokens_in():
        for copy in tokens_out:
            copy.wait_recv()

    def widen(j, c):
        if c == 0:
            weights[j][0].wait()
            weights[j][1].wait()
        n = HID // BLOCKS
        cols = slice(c * n, (c + 1) * n)
        block = xall[...].reshape(G * T, D)
        gate = jnp.dot(block, wg[j, :, cols], preferred_element_type=F32)
        up = jnp.dot(block, wu[j, :, cols], preferred_element_type=F32)
        hid[:, cols] = (jax.nn.gelu(gate) * up).astype(BF16)

    def narrow(j):
        weights[j][2].wait()
        weight = call[...].reshape(G * T, LANES)
        lanes = lax.broadcasted_iota(jnp.int32, (G * T, LANES), 1)
        weight = jnp.sum(jnp.where(lanes == e * L + j, weight, 0.0), axis=1, keepdims=True)
        for c in range(BLOCKS):
            cols = slice(c * (D // BLOCKS), (c + 1) * (D // BLOCKS))
            out = jnp.dot(hid[...], wd[j, :, cols], preferred_element_type=F32)
            out = weight * out.astype(BF16).astype(F32)
            if j == 0:
                acc[:, cols] = out
            else:
                acc[:, cols] += out

    back = []
    for k in range(1, G):
        back.append(remote(po.at[k], pi.at[k], p_send.at[k], p_recv.at[k],
                           dev(p, lax.rem(e + G - k, G), d)))
    onward = remote(mixed, landed, h_sem.at[0], h_sem.at[1], dev(after, e, d))

    def give_back():
        for k in range(1, G):
            po[k] = acc[k * T:(k + 1) * T, :].astype(BF16)
            back[k - 1].start()

    def hand_on():
        total = tok_ref[...].astype(F32) + acc[0:T, :]
        for k, copy in enumerate(back):
            copy.wait_recv()
            total = total + pi[k + 1].astype(F32)
        mixed[...] = total.astype(BF16)
        onward.start()

    C = len(spans)

    def sent(c):
        for g in range(G):
            stage(c, g).wait_send()
        for to in range(1, Z - 1):
            @pl.when(d != to)
            def _():
                gather(c, d, to).wait_send()

    def parts_sent():
        @pl.when(is_adj)
        def _():
            for m in range(len(messages)):
                onto_end(m).wait_send()

    def route_rows():
        small[2].wait()
        for g in range(G):
            placed = jnp.dot(maps[g][0] + maps[g][1], nb_ref[...],
                             preferred_element_type=F32).astype(BF16)
            for t in range(NTT):
                ns[g, place_of(t)] = placed[:, t * LANES:(t + 1) * LANES]

    def out(c):
        route(c)
        send_stage(c)

    M = len(messages)
    extra = M - C

    small[1].wait()
    route(0)
    pl.semaphore_wait(barrier, len(peers))
    send_stage(0)
    route_rows()
    send_rows(0)
    out(1)
    if QS > 1:
        send_rows(1)
    out(2)
    out(3)
    out(4)
    out(5)
    combine(0)
    combine_rows(0)
    out(6)
    out(7)
    send_rows(Q - 1)
    forward_tokens()
    combine(1)
    if QS > 1:
        combine_rows(1)
    combine(2)
    rows_for_end(0)
    reduce(0)
    combine(3)
    reduce(1)
    if QS > 1:
        rows_for_end(1)
        reduce(2)
    combine(4)
    reduce(2 + extra)
    tokens_in()
    widen(0, 0)
    combine(5)
    reduce(3 + extra)
    widen(0, 1)
    widen(0, 2)
    combine(6)
    reduce(4 + extra)
    narrow(0)
    if L > 1:
        widen(1, 0)
    combine(7)
    reduce(5 + extra)
    if L > 1:
        widen(1, 1)
        widen(1, 2)
    reduce(6 + extra)
    if L > 1:
        narrow(1)
    give_back()
    combine_rows(Q - 1)
    rows_for_own()
    reduce(7 + extra)
    hand_on()
    for c in range(C):
        own_wait(c)
    for u in range(0, U, 2):
        own_term(u, 2)
    for c in range(C):
        sent(c)
    wait_rows_sent()
    for copy in tokens_out + back:
        copy.wait_send()
    onward.wait_recv()
    ho_ref[...] = landed[...]
    onward.wait_send()
    for m in range(M):
        add_part(m)
    parts_sent()


def write_out(handed_ref, grad_ref, handed_hbm, grad_hbm, sem):
    L, DZ = grad_ref.shape[:2]
    half = DZ // 2
    copies = [pltpu.make_async_copy(handed_ref, handed_hbm, sem.at[0])]
    for j in range(L):
        for i in range(2):
            at = (j, pl.ds(i * half, half))
            copies.append(pltpu.make_async_copy(
                grad_ref.at[at], grad_hbm.at[at], sem.at[1 + 2 * j + i]))
    for copy in copies:
        copy.start()
    for copy in copies:
        copy.wait()


def shards(
    acts_fwd, ids_fwd, norm_gain, router_w, gate_w, up_w, down_w, normed_bwd, ids_bwd, dgate_bwd
):
    S, G, Z = lax.axis_size("pipe"), lax.axis_size("expert"), lax.axis_size("dp")
    L = gate_w.shape[1]
    E = G * L
    T, D = acts_fwd.shape[2:]
    HID = gate_w.shape[3]
    U = HID // LANES
    C = len(CHUNKS)
    DZ = D // Z
    R = L * CAP
    FR = G * R
    W = max(-(-(s + 1) * R // TILE) * TILE - s * R // TILE * TILE for s in range(G))
    NTT = D // LANES
    N1, NT = window_sizes(D, Z)
    M = len(message_plan(L * min(DZ, LANES), L * (DZ - min(DZ, LANES)))[0])
    vmem = pl.BlockSpec(memory_space=pltpu.VMEM)
    hbm = pl.BlockSpec(memory_space=pltpu.HBM)
    dma = pltpu.SemaphoreType.DMA
    V = pltpu.VMEM
    handed, grad = pl.pallas_call(
        functools.partial(relay_kernel, (S, G, Z, L)),
        out_shape=(jax.ShapeDtypeStruct((T, D), BF16), jax.ShapeDtypeStruct((L, DZ, HID), F32)),
        in_specs=[hbm] * 10,
        out_specs=(vmem, vmem),
        scratch_shapes=[
            V((T, D), BF16), V((2, T), jnp.int32), V((1, D), F32), V((E, D), BF16),
            V((T, D), BF16), V((2, T), jnp.int32), V((T, 2, HID), BF16), dma((7,)),
            V((L, D, HID), BF16), V((L, D, HID), BF16), V((L, HID, D), BF16),
            V((G, U, W, LANES), BF16), V((G, U, W, LANES), BF16), V((Z, U, FR, LANES), BF16),
            V((G, NTT, W, LANES), BF16), V((G, NTT, W, LANES), BF16),
            V((Z, NTT, FR, LANES), BF16), V((NT * LANES, Z * FR), F32),
            V((L * DZ, (Z - 1) * FR), BF16), V((L * DZ, Z * FR), BF16), V((L * DZ, FR), BF16),
            V((U, L * DZ, LANES), BF16), V((U, L * DZ, LANES), BF16),
            V((G, T, D), BF16), V((G, T, LANES), F32), V((G * T, HID), BF16), V((G * T, D), F32),
            V((G, T, D), BF16), V((G, T, D), BF16), V((T, D), BF16), V((T, D), BF16),
            dma((L, 3)), dma((C, G)), dma((C, G)), dma((3, G)), dma((3, G)), dma((NTT, Z)), dma((NTT, Z)),
            dma((C, Z)), dma((C, Z)), dma((M,)), dma((M,)),
            dma((G,)), dma((G,)), dma((G,)), dma((G,)), dma((G,)), dma((G,)), dma((2,)),
        ],
        compiler_params=pltpu.CompilerParams(
            collective_id=0, has_side_effects=True, vmem_limit_bytes=36 << 20),
    )(*(pltpu.with_memory_space_constraint(x, pltpu.HBM) for x in (
        acts_fwd[0, 0], ids_fwd[0, 0].T, norm_gain, router_w[0].T, gate_w[0], up_w[0], down_w[0],
        normed_bwd[0, 0], ids_bwd[0, 0].T, dgate_bwd[0, 0],
    )))
    handed, grad = pl.pallas_call(
        write_out,
        out_shape=(jax.ShapeDtypeStruct((T, D), BF16), jax.ShapeDtypeStruct((L, DZ, HID), F32)),
        in_specs=[vmem] * 2,
        out_specs=[pl.BlockSpec(memory_space=pl.ANY)] * 2,
        scratch_shapes=[dma((1 + 2 * L,))],
        compiler_params=pltpu.CompilerParams(vmem_limit_bytes=1 << 20),
    )(handed, grad)
    return handed[None, None], grad[None]


def solution(mesh):
    in_specs = (
        P("pipe", "dp", "expert", None),
        P("pipe", "dp", "expert", None),
        P("pipe", None),
        P("pipe", None, None),
        P("pipe", "expert", None, None),
        P("pipe", "expert", None, None),
        P("pipe", "expert", None, None),
        P("pipe", "dp", "expert", None),
        P("pipe", "dp", "expert", None),
        P("pipe", "dp", "expert", None, None),
    )
    out_specs = (P("pipe", "dp", "expert", None), P("pipe", "expert", "dp", None))
    return jax.shard_map(shards, mesh=mesh, in_specs=in_specs, out_specs=out_specs, check_vma=False)
```

```python
import functools

import jax
import jax.numpy as jnp
from jax import lax
from jax.experimental import pallas as pl
from jax.experimental.pallas import tpu as pltpu
from jax.sharding import PartitionSpec as P

CAP = 36
TILE = 16
LANES = 128
BLOCKS = 3
CHUNKS = (1, 1, 1, 1, 2, 2, 2, 2)
F32 = jnp.float32
BF16 = jnp.bfloat16


def window_sizes(D, Z):
    DZ = D // Z
    end = -(-DZ // LANES)
    pair = max(-(-(b + 2) * DZ // LANES) - b * DZ // LANES for b in range(0, Z, 2))
    return end, pair


def message_plan(a, b):
    if not b:
        messages, at = [], 0
        for n in CHUNKS:
            messages.append((at, n, 0, a))
            at += n
        return messages, [[c] for c in range(len(CHUNKS))]
    messages, at = [(0, 1, 0, a), (1, 1, 0, a), (0, 2, a, b)], 2
    fresh = [[0], [1], []]
    for c, n in enumerate(CHUNKS):
        if c >= 2:
            messages.append((at, n, 0, a + b))
            fresh.append([c])
            at += n
    return messages, fresh


def relay_kernel(
    dims,
    tok_hbm, idf_hbm, gain_hbm, router_hbm, wg_hbm, wu_hbm, wd_hbm, nb_hbm, idb_hbm, dg_hbm,
    ho_ref, grad_ref,
    tok_ref, idf_ref, gain_ref, router_ref, nb_ref, idb_ref, dg_ref, in_sem,
    wg, wu, wd, gs, st, gall, ns, stn, nall, turned, lhs_red, lhs_own, lhs_end, ps, rp,
    xall, call, hid, acc, po, pi, mixed, landed,
    w_sem, s_send, s_recv, n_send, n_recv, nz_send, nz_recv, z_send, z_recv, r_send, r_recv,
    x_send, x_recv, c_send, c_recv, p_send, p_recv, h_sem,
):
    S, G, Z, L = dims
    T, D = tok_ref.shape
    HID = dg_ref.shape[2]
    U = HID // LANES
    DZ = D // Z
    R = L * CAP
    FR = G * R
    W = gs.shape[2]
    NTT = D // LANES
    N1, NT = window_sizes(D, Z)
    NA = min(DZ, LANES)
    NB = DZ - NA
    QS = 2 if NB else 1
    starts = [s * R // TILE * TILE for s in range(G)]
    p = lax.axis_index("pipe")
    e = lax.axis_index("expert")
    d = lax.axis_index("dp")
    mirror = S - 1 - p
    after = lax.rem(p + 1, S)
    before = lax.rem(p + S - 1, S)
    first = d == 0
    last = d == Z - 1
    is_end = first | last
    is_mid = (d > 0) & (d < Z - 1)
    is_adj = (d == 1) | (d == Z - 2)
    side = jnp.where(d < Z // 2, 0, 1)
    low = jnp.where(d == 1, 1, 0)
    end_row = pl.multiple_of(side * ((Z - 1) * DZ - LANES * (NTT - N1)), 8)
    own_row = pl.multiple_of(d * DZ - (d // 2 * 2 * DZ) // LANES * LANES, 8)
    end_dev = jnp.where(d == 1, 0, Z - 1)

    def dev(pp, ee, dd):
        return {"pipe": pp, "expert": ee, "dp": dd}

    def remote(src, dst, ss, rs, to):
        return pltpu.make_async_remote_copy(
            src_ref=src, dst_ref=dst, send_sem=ss, recv_sem=rs,
            device_id=to, device_id_type=pl.DeviceIdType.MESH)

    def local(src, dst, sem):
        return pltpu.make_async_copy(src, dst, sem)

    small = []
    for i, (src, dst) in enumerate((
        (idb_hbm, idb_ref), (dg_hbm, dg_ref), (nb_hbm, nb_ref), (tok_hbm, tok_ref),
        (idf_hbm, idf_ref), (gain_hbm, gain_ref), (router_hbm, router_ref),
    )):
        copy = local(src, dst, in_sem.at[i])
        copy.start()
        small.append(copy)

    barrier = pltpu.get_barrier_semaphore()
    peers = [dev(mirror, g, d) for g in range(G)]
    peers += [dev(p, lax.rem(e + k, G), d) for k in range(1, G)]
    peers += [dev(p, e, lax.rem(d + k, Z)) for k in range(1, Z)]
    peers += [dev(after, e, d), dev(before, e, d)]
    for peer in peers:
        pl.semaphore_signal(barrier, inc=1, device_id=peer, device_id_type=pl.DeviceIdType.MESH)

    weights = []
    for j in range(L):
        trio = [local(wg_hbm.at[j], wg.at[j], w_sem.at[j, 0]),
                local(wu_hbm.at[j], wu.at[j], w_sem.at[j, 1]),
                local(wd_hbm.at[j], wd.at[j], w_sem.at[j, 2])]
        for copy in trio:
            copy.start()
        weights.append(trio)

    small[0].wait()
    ids = [idb_ref[k:k + 1, :].astype(F32) for k in range(2)]
    labels = lax.broadcasted_iota(jnp.int32, (8, T), 0).astype(F32)
    onehot = [jnp.where(ids[k] == labels, 1.0, 0.0) for k in range(2)]
    earlier = lax.broadcasted_iota(jnp.int32, (T, T), 0) < lax.broadcasted_iota(
        jnp.int32, (T, T), 1)
    earlier = jnp.where(earlier, 1.0, 0.0).astype(BF16)
    counts = [jnp.dot(onehot[k].astype(BF16), earlier, preferred_element_type=F32)
              for k in range(2)]
    counts[1] = counts[1] + jnp.sum(onehot[0], axis=1, keepdims=True)
    rank = [jnp.sum(counts[k] * onehot[k], axis=0, keepdims=True) for k in range(2)]
    shift = lax.rem(e * R, TILE).astype(F32)
    slots = lax.broadcasted_iota(jnp.int32, (W, T), 0).astype(F32)
    maps = []
    for g in range(G):
        pair = []
        for k in range(2):
            own = jnp.where((ids[k] >= g * L) & (ids[k] < (g + 1) * L),
                            shift + (ids[k] - g * L) * CAP + rank[k], -1.0)
            pair.append(jnp.where(slots == own, 1.0, 0.0).astype(BF16))
        maps.append(pair)
    both = jnp.concatenate([jnp.concatenate(pair, axis=1) for pair in maps], axis=0)

    spans = []
    at = 0
    for n in CHUNKS:
        spans.append((at, n))
        at += n
    assert at == U
    messages, fresh = message_plan(L * NA, L * NB)

    def units(ref, c):
        return ref.at[pl.ds(spans[c][0], spans[c][1])]

    def stage(c, g):
        return remote(units(gs.at[g], c), units(st.at[e], c), s_send.at[c, g], s_recv.at[c, e],
                      dev(mirror, g, d))

    def route(c):
        u, n = spans[c]
        cols = slice(u * LANES, (u + n) * LANES)
        picked = jnp.concatenate([dg_ref[:, 0, cols], dg_ref[:, 1, cols]], axis=0)
        placed = jnp.dot(both, picked, preferred_element_type=F32).astype(BF16)
        for g in range(G):
            for i in range(n):
                gs[g, u + i] = placed[g * W:(g + 1) * W, i * LANES:(i + 1) * LANES]

    def send_stage(c):
        for g in range(G):
            stage(c, g).start()

    bounds = [0, 2, 2 * N1, NTT] if QS > 1 else [0, 2, NTT]
    Q = len(bounds) - 1

    def rows_stage(q, g):
        span = pl.ds(bounds[q], bounds[q + 1] - bounds[q])
        return remote(ns.at[g, span], stn.at[e, span], n_send.at[q, g], n_recv.at[q, e],
                      dev(mirror, g, d))

    def send_rows(q):
        for g in range(G):
            rows_stage(q, g).start()

    def window(b):
        lo = b // 2 * 2 * DZ // LANES
        return range(lo, min(lo + NT, NTT))

    def place_of(t):
        return 2 * t if t < NTT // 2 else 2 * (NTT - 1 - t) + 1

    def rows_gather(i, r, to):
        return remote(nall.at[r, i], nall.at[r, i], nz_send.at[i, to], nz_recv.at[i, r],
                      dev(p, e, to))

    def rows_dests(i):
        return [b for b in range(1, Z - 1) if i in [place_of(t) for t in window(b)]]

    def combine_rows(q):
        for s in range(G):
            span = pl.ds(bounds[q], bounds[q + 1] - bounds[q])
            remote(ns.at[0, span], stn.at[s, span], n_send.at[q, 0], n_recv.at[q, s],
                   dev(mirror, 0, d)).wait_recv()
        for i in range(bounds[q], bounds[q + 1]):
            for row in range(0, FR, TILE):
                parts = [stn[s, i, row - starts[s]:row - starts[s] + TILE, :] for s in range(G)
                         if starts[s] <= row < starts[s] + W]
                nall[d, i, row:row + TILE, :] = functools.reduce(lambda a, b: a + b, parts)
            for to in rows_dests(i):
                @pl.when(d != to)
                def _():
                    rows_gather(i, d, to).start()

    def rows_arrive(i, r):
        rows_gather(i, r, 1).wait_recv()

    def wait_rows_sent():
        for q in range(Q):
            for g in range(G):
                rows_stage(q, g).wait_send()
        for i in range(NTT):
            for to in rows_dests(i):
                @pl.when(d != to)
                def _():
                    rows_gather(i, d, to).wait_send()

    def gather(c, r, to):
        return remote(units(gall.at[r], c), units(gall.at[r], c), z_send.at[c, to],
                      z_recv.at[c, r], dev(p, e, to))

    def combine(c):
        for s in range(G):
            remote(units(gs.at[0], c), units(st.at[s], c), s_send.at[c, 0], s_recv.at[c, s],
                   dev(mirror, 0, d)).wait_recv()
        u, n = spans[c]
        for v in range(u, u + n):
            for i in range(0, FR, TILE):
                parts = [st[s, v, i - starts[s]:i - starts[s] + TILE, :] for s in range(G)
                         if starts[s] <= i < starts[s] + W]
                gall[d, v, i:i + TILE, :] = functools.reduce(lambda a, b: a + b, parts)
        order = [Z - 2, 1] + list(range(2, Z - 2))
        for to in order:
            @pl.when((d != to) & first)
            def _():
                gather(c, d, to).start()
        order[0:2] = [1, Z - 2]
        for to in order:
            @pl.when((d != to) & (d > 0))
            def _():
                gather(c, d, to).start()

    def mask_into(lhs, at, row, n, height):
        whole = turned[pl.ds(pl.multiple_of(row, 8), n), 0:height]
        place = lax.rem(lax.broadcasted_iota(jnp.int32, (1, height), 1), R)
        for j in range(L):
            mine = (place >= j * CAP) & (place < (j + 1) * CAP)
            lhs[at + j * n:at + (j + 1) * n, :] = jnp.where(mine, whole, 0.0).astype(BF16)

    def turn(t, block):
        turned[t * LANES:(t + 1) * LANES, 0:block.shape[0]] = block.astype(F32).T

    def rows_for_end(q):
        at, n = [(0, NA), (L * NA, NB)][q]
        i = 2 * q + side

        @pl.when(is_adj)
        def _():
            for k in range(Z - 1):
                @pl.when(low + k != d)
                def _():
                    rows_arrive(i, low + k)
            turn(0, nall[pl.ds(low, Z - 1), i].reshape((Z - 1) * FR, LANES))
            mask_into(lhs_red, at, side * (LANES - n), n, (Z - 1) * FR)

    def rows_for_own():
        for b in range(1, Z - 1):
            @pl.when(d == b)
            def _():
                for t in window(b):
                    i = place_of(t)
                    early = b in (1, Z - 2) and i in range(int(b != 1), 2 * QS, 2)
                    for r in range(Z):
                        if r != b and not (early and r != (0 if b == 1 else Z - 1)):
                            rows_arrive(i, r)
                for k, t in enumerate(window(b)):
                    turn(k, nall[:, place_of(t)].reshape(Z * FR, LANES))
                mask_into(lhs_own, 0, own_row, DZ, Z * FR)
        for b in (0, Z - 1):
            @pl.when(d == b)
            def _():
                for k in range(N1):
                    t = k if b == 0 else NTT - N1 + k
                    turn(k, nall[b, place_of(t)])
                mask_into(lhs_end, 0, end_row, DZ, FR)

    def block_arrives(c, r):
        return gather(c, r, 1)

    def onto_end(m):
        u, n, lo, h = messages[m]
        at = (pl.ds(u, n), pl.ds(lo, h))
        return remote(ps.at[at], rp.at[at], r_send.at[m], r_recv.at[m], dev(p, e, end_dev))

    def reduce(m):
        u, n, lo, h = messages[m]

        @pl.when(is_adj)
        def _():
            for c in fresh[m]:
                for i in range(Z - 1):
                    @pl.when(low + i != d)
                    def _():
                        block_arrives(c, low + i).wait_recv()
            block = jnp.concatenate(
                [gall[pl.ds(low, Z - 1), u + i].reshape((Z - 1) * FR, LANES) for i in range(n)],
                axis=1)
            part = jnp.dot(lhs_red[lo:lo + h, :], block, preferred_element_type=F32).astype(BF16)
            for i in range(n):
                ps[u + i, lo:lo + h, :] = part[:, i * LANES:(i + 1) * LANES]
            onto_end(m).start()

    def own_wait(c):
        @pl.when(is_adj)
        def _():
            block_arrives(c, jnp.where(d == 1, 0, Z - 1)).wait_recv()
        if Z > 4:
            @pl.when(is_mid & jnp.logical_not(is_adj))
            def _():
                for r in range(Z):
                    @pl.when(d != r)
                    def _():
                        block_arrives(c, r).wait_recv()

    def own_term(u, n):
        cols = slice(u * LANES, (u + n) * LANES)

        @pl.when(is_mid)
        def _():
            block = jnp.concatenate(
                [gall[:, u + i].reshape(Z * FR, LANES) for i in range(n)], axis=1)
            whole = jnp.dot(lhs_own[...], block, preferred_element_type=F32)
            for j in range(L):
                grad_ref[j, :, cols] = whole[j * DZ:(j + 1) * DZ]

        @pl.when(is_end)
        def _():
            block = jnp.concatenate([gall[d, u + i] for i in range(n)], axis=1)
            whole = jnp.dot(lhs_end[...], block, preferred_element_type=F32)
            for j in range(L):
                grad_ref[j, :, cols] = whole[j * DZ:(j + 1) * DZ]

    def add_part(m):
        u, n, lo, h = messages[m]

        @pl.when(is_end)
        def _():
            onto_end(m).wait_recv()
            for i in range(u, u + n):
                cols = slice(i * LANES, (i + 1) * LANES)
                for at, size, row in ((0, NA, side * NB), (L * NA, NB, (1 - side) * NA)):
                    if size and lo <= at < lo + h:
                        for j in range(L):
                            rows_of = pl.ds(pl.multiple_of(row, 8), size)
                            grad_ref[j, rows_of, cols] += rp[
                                i, at + j * size:at + (j + 1) * size].astype(F32)

    def forward_tokens():
        for copy in small[3:]:
            copy.wait()
        tokens = tok_ref[...].astype(F32)
        inv = lax.rsqrt(jnp.mean(tokens * tokens, axis=-1, keepdims=True) + 1e-05)
        normed = (tokens * inv * gain_ref[...]).astype(BF16)
        logits = lax.dot_general(normed, router_ref[...], (((1,), (1,)), ((), ())),
                                 preferred_element_type=F32)
        lane_e = lax.broadcasted_iota(jnp.int32, logits.shape, 1).astype(F32)
        diagonal = lax.broadcasted_iota(jnp.int32, (T, T), 0) == lax.broadcasted_iota(
            jnp.int32, (T, T), 1)
        one, two = [
            jnp.sum(jnp.where(diagonal, idf_ref[k:k + 1, :].astype(F32), 0.0), axis=1,
                    keepdims=True)
            for k in range(2)]
        l0 = jnp.sum(jnp.where(lane_e == one, logits, 0.0), axis=1, keepdims=True)
        l1 = jnp.sum(jnp.where(lane_e == two, logits, 0.0), axis=1, keepdims=True)
        lane = lax.broadcasted_iota(jnp.int32, (T, LANES), 1).astype(F32)
        xall[0] = normed
        call[0] = jnp.where(lane == one, jax.nn.sigmoid(l0 - l1), 0.0) + jnp.where(
            lane == two, jax.nn.sigmoid(l1 - l0), 0.0)
        for copy in tokens_out:
            copy.start()

    tokens_out = []
    for k in range(1, G):
        to = dev(p, lax.rem(e + k, G), d)
        tokens_out += [remote(xall.at[0], xall.at[k], x_send.at[k], x_recv.at[k], to),
                       remote(call.at[0], call.at[k], c_send.at[k], c_recv.at[k], to)]

    def tokens_in():
        for copy in tokens_out:
            copy.wait_recv()

    def widen(j, c):
        if c == 0:
            weights[j][0].wait()
            weights[j][1].wait()
        n = HID // BLOCKS
        cols = slice(c * n, (c + 1) * n)
        block = xall[...].reshape(G * T, D)
        gate = jnp.dot(block, wg[j, :, cols], preferred_element_type=F32)
        up = jnp.dot(block, wu[j, :, cols], preferred_element_type=F32)
        hid[:, cols] = (jax.nn.gelu(gate) * up).astype(BF16)

    def narrow(j):
        weights[j][2].wait()
        weight = call[...].reshape(G * T, LANES)
        lanes = lax.broadcasted_iota(jnp.int32, (G * T, LANES), 1)
        weight = jnp.sum(jnp.where(lanes == e * L + j, weight, 0.0), axis=1, keepdims=True)
        for c in range(BLOCKS):
            cols = slice(c * (D // BLOCKS), (c + 1) * (D // BLOCKS))
            out = jnp.dot(hid[...], wd[j, :, cols], preferred_element_type=F32)
            out = weight * out.astype(BF16).astype(F32)
            if j == 0:
                acc[:, cols] = out
            else:
                acc[:, cols] += out

    back = []
    for k in range(1, G):
        back.append(remote(po.at[k], pi.at[k], p_send.at[k], p_recv.at[k],
                           dev(p, lax.rem(e + G - k, G), d)))
    onward = remote(mixed, landed, h_sem.at[0], h_sem.at[1], dev(after, e, d))

    def give_back():
        for k in range(1, G):
            po[k] = acc[k * T:(k + 1) * T, :].astype(BF16)
            back[k - 1].start()

    def hand_on():
        total = tok_ref[...].astype(F32) + acc[0:T, :]
        for k, copy in enumerate(back):
            copy.wait_recv()
            total = total + pi[k + 1].astype(F32)
        mixed[...] = total.astype(BF16)
        onward.start()

    C = len(spans)

    def sent(c):
        for g in range(G):
            stage(c, g).wait_send()
        for to in range(1, Z - 1):
            @pl.when(d != to)
            def _():
                gather(c, d, to).wait_send()

    def parts_sent():
        @pl.when(is_adj)
        def _():
            for m in range(len(messages)):
                onto_end(m).wait_send()

    def route_rows():
        small[2].wait()
        for g in range(G):
            placed = jnp.dot(maps[g][0] + maps[g][1], nb_ref[...],
                             preferred_element_type=F32).astype(BF16)
            for t in range(NTT):
                ns[g, place_of(t)] = placed[:, t * LANES:(t + 1) * LANES]

    def out(c):
        route(c)
        send_stage(c)

    M = len(messages)
    extra = M - C

    small[1].wait()
    route(0)
    pl.semaphore_wait(barrier, len(peers))
    send_stage(0)
    route_rows()
    send_rows(0)
    out(1)
    if QS > 1:
        send_rows(1)
    out(2)
    out(3)
    out(4)
    out(5)
    combine(0)
    forward_tokens()
    combine_rows(0)
    out(6)
    out(7)
    send_rows(Q - 1)
    combine(1)
    if QS > 1:
        combine_rows(1)
    combine(2)
    rows_for_end(0)
    reduce(0)
    combine(3)
    reduce(1)
    if QS > 1:
        rows_for_end(1)
        reduce(2)
    combine(4)
    reduce(2 + extra)
    tokens_in()
    widen(0, 0)
    combine(5)
    reduce(3 + extra)
    widen(0, 1)
    widen(0, 2)
    combine(6)
    reduce(4 + extra)
    narrow(0)
    if L > 1:
        widen(1, 0)
    combine(7)
    reduce(5 + extra)
    if L > 1:
        widen(1, 1)
        widen(1, 2)
    reduce(6 + extra)
    if L > 1:
        narrow(1)
    give_back()
    combine_rows(Q - 1)
    rows_for_own()
    reduce(7 + extra)
    hand_on()
    for c in range(C):
        own_wait(c)
    for u in range(0, U, 2):
        own_term(u, 2)
    for c in range(C):
        sent(c)
    wait_rows_sent()
    for copy in tokens_out + back:
        copy.wait_send()
    onward.wait_recv()
    ho_ref[...] = landed[...]
    onward.wait_send()
    for m in range(M):
        add_part(m)
    parts_sent()


def write_out(handed_ref, grad_ref, handed_hbm, grad_hbm, sem):
    L, DZ = grad_ref.shape[:2]
    half = DZ // 2
    copies = [pltpu.make_async_copy(handed_ref, handed_hbm, sem.at[0])]
    for j in range(L):
        for i in range(2):
            at = (j, pl.ds(i * half, half))
            copies.append(pltpu.make_async_copy(
                grad_ref.at[at], grad_hbm.at[at], sem.at[1 + 2 * j + i]))
    for copy in copies:
        copy.start()
    for copy in copies:
        copy.wait()


def shards(
    acts_fwd, ids_fwd, norm_gain, router_w, gate_w, up_w, down_w, normed_bwd, ids_bwd, dgate_bwd
):
    S, G, Z = lax.axis_size("pipe"), lax.axis_size("expert"), lax.axis_size("dp")
    L = gate_w.shape[1]
    E = G * L
    T, D = acts_fwd.shape[2:]
    HID = gate_w.shape[3]
    U = HID // LANES
    C = len(CHUNKS)
    DZ = D // Z
    R = L * CAP
    FR = G * R
    W = max(-(-(s + 1) * R // TILE) * TILE - s * R // TILE * TILE for s in range(G))
    NTT = D // LANES
    N1, NT = window_sizes(D, Z)
    M = len(message_plan(L * min(DZ, LANES), L * (DZ - min(DZ, LANES)))[0])
    vmem = pl.BlockSpec(memory_space=pltpu.VMEM)
    hbm = pl.BlockSpec(memory_space=pltpu.HBM)
    dma = pltpu.SemaphoreType.DMA
    V = pltpu.VMEM
    handed, grad = pl.pallas_call(
        functools.partial(relay_kernel, (S, G, Z, L)),
        out_shape=(jax.ShapeDtypeStruct((T, D), BF16), jax.ShapeDtypeStruct((L, DZ, HID), F32)),
        in_specs=[hbm] * 10,
        out_specs=(vmem, vmem),
        scratch_shapes=[
            V((T, D), BF16), V((2, T), jnp.int32), V((1, D), F32), V((E, D), BF16),
            V((T, D), BF16), V((2, T), jnp.int32), V((T, 2, HID), BF16), dma((7,)),
            V((L, D, HID), BF16), V((L, D, HID), BF16), V((L, HID, D), BF16),
            V((G, U, W, LANES), BF16), V((G, U, W, LANES), BF16), V((Z, U, FR, LANES), BF16),
            V((G, NTT, W, LANES), BF16), V((G, NTT, W, LANES), BF16),
            V((Z, NTT, FR, LANES), BF16), V((NT * LANES, Z * FR), F32),
            V((L * DZ, (Z - 1) * FR), BF16), V((L * DZ, Z * FR), BF16), V((L * DZ, FR), BF16),
            V((U, L * DZ, LANES), BF16), V((U, L * DZ, LANES), BF16),
            V((G, T, D), BF16), V((G, T, LANES), F32), V((G * T, HID), BF16), V((G * T, D), F32),
            V((G, T, D), BF16), V((G, T, D), BF16), V((T, D), BF16), V((T, D), BF16),
            dma((L, 3)), dma((C, G)), dma((C, G)), dma((3, G)), dma((3, G)), dma((NTT, Z)), dma((NTT, Z)),
            dma((C, Z)), dma((C, Z)), dma((M,)), dma((M,)),
            dma((G,)), dma((G,)), dma((G,)), dma((G,)), dma((G,)), dma((G,)), dma((2,)),
        ],
        compiler_params=pltpu.CompilerParams(
            collective_id=0, has_side_effects=True, vmem_limit_bytes=36 << 20),
    )(*(pltpu.with_memory_space_constraint(x, pltpu.HBM) for x in (
        acts_fwd[0, 0], ids_fwd[0, 0].T, norm_gain, router_w[0].T, gate_w[0], up_w[0], down_w[0],
        normed_bwd[0, 0], ids_bwd[0, 0].T, dgate_bwd[0, 0],
    )))
    handed, grad = pl.pallas_call(
        write_out,
        out_shape=(jax.ShapeDtypeStruct((T, D), BF16), jax.ShapeDtypeStruct((L, DZ, HID), F32)),
        in_specs=[vmem] * 2,
        out_specs=[pl.BlockSpec(memory_space=pl.ANY)] * 2,
        scratch_shapes=[dma((1 + 2 * L,))],
        compiler_params=pltpu.CompilerParams(vmem_limit_bytes=1 << 20),
    )(handed, grad)
    return handed[None, None], grad[None]


def solution(mesh):
    in_specs = (
        P("pipe", "dp", "expert", None),
        P("pipe", "dp", "expert", None),
        P("pipe", None),
        P("pipe", None, None),
        P("pipe", "expert", None, None),
        P("pipe", "expert", None, None),
        P("pipe", "expert", None, None),
        P("pipe", "dp", "expert", None),
        P("pipe", "dp", "expert", None),
        P("pipe", "dp", "expert", None, None),
    )
    out_specs = (P("pipe", "dp", "expert", None), P("pipe", "expert", "dp", None))
    return jax.shard_map(shards, mesh=mesh, in_specs=in_specs, out_specs=out_specs, check_vma=False)
```

```python
import functools

import jax
import jax.numpy as jnp
from jax import lax
from jax.experimental import pallas as pl
from jax.experimental.pallas import tpu as pltpu
from jax.sharding import PartitionSpec as P

CAP = 36
TILE = 16
LANES = 128
BLOCKS = 3
CHUNKS = (1, 1, 1, 1, 2, 2, 2, 2)
F32 = jnp.float32
BF16 = jnp.bfloat16


def window_sizes(D, Z):
    DZ = D // Z
    end = -(-DZ // LANES)
    pair = max(-(-(b + 2) * DZ // LANES) - b * DZ // LANES for b in range(0, Z, 2))
    return end, pair


def message_plan(a, b):
    if not b:
        messages, at = [], 0
        for n in CHUNKS:
            messages.append((at, n, 0, a))
            at += n
        return messages, [[c] for c in range(len(CHUNKS))]
    messages, at = [(0, 1, 0, a), (1, 1, 0, a), (0, 2, a, b)], 2
    fresh = [[0], [1], []]
    for c, n in enumerate(CHUNKS):
        if c >= 2:
            messages.append((at, n, 0, a + b))
            fresh.append([c])
            at += n
    return messages, fresh


def relay_kernel(
    dims,
    tok_hbm, idf_hbm, gain_hbm, router_hbm, wg_hbm, wu_hbm, wd_hbm, nb_hbm, idb_hbm, dg_hbm,
    ho_ref, grad_ref,
    tok_ref, idf_ref, gain_ref, router_ref, nb_ref, idb_ref, dg_ref, in_sem,
    wg, wu, wd, gs, st, gall, ns, stn, nall, turned, lhs_red, lhs_own, lhs_end, ps, rp,
    xall, call, hid, acc, po, pi, mixed, landed,
    w_sem, s_send, s_recv, n_send, n_recv, nz_send, nz_recv, z_send, z_recv, r_send, r_recv,
    x_send, x_recv, c_send, c_recv, p_send, p_recv, h_sem,
):
    S, G, Z, L = dims
    T, D = tok_ref.shape
    HID = dg_ref.shape[2]
    U = HID // LANES
    DZ = D // Z
    R = L * CAP
    FR = G * R
    W = gs.shape[2]
    NTT = D // LANES
    N1, NT = window_sizes(D, Z)
    NA = min(DZ, LANES)
    NB = DZ - NA
    QS = 2 if NB else 1
    starts = [s * R // TILE * TILE for s in range(G)]
    p = lax.axis_index("pipe")
    e = lax.axis_index("expert")
    d = lax.axis_index("dp")
    mirror = S - 1 - p
    after = lax.rem(p + 1, S)
    before = lax.rem(p + S - 1, S)
    first = d == 0
    last = d == Z - 1
    is_end = first | last
    is_mid = (d > 0) & (d < Z - 1)
    is_adj = (d == 1) | (d == Z - 2)
    side = jnp.where(d < Z // 2, 0, 1)
    low = jnp.where(d == 1, 1, 0)
    end_row = pl.multiple_of(side * ((Z - 1) * DZ - LANES * (NTT - N1)), 8)
    own_row = pl.multiple_of(d * DZ - (d // 2 * 2 * DZ) // LANES * LANES, 8)
    end_dev = jnp.where(d == 1, 0, Z - 1)

    def dev(pp, ee, dd):
        return {"pipe": pp, "expert": ee, "dp": dd}

    def remote(src, dst, ss, rs, to):
        return pltpu.make_async_remote_copy(
            src_ref=src, dst_ref=dst, send_sem=ss, recv_sem=rs,
            device_id=to, device_id_type=pl.DeviceIdType.MESH)

    def local(src, dst, sem):
        return pltpu.make_async_copy(src, dst, sem)

    small = []
    for i, (src, dst) in enumerate((
        (idb_hbm, idb_ref), (dg_hbm, dg_ref), (nb_hbm, nb_ref), (tok_hbm, tok_ref),
        (idf_hbm, idf_ref), (gain_hbm, gain_ref), (router_hbm, router_ref),
    )):
        copy = local(src, dst, in_sem.at[i])
        copy.start()
        small.append(copy)

    barrier = pltpu.get_barrier_semaphore()
    peers = [dev(mirror, g, d) for g in range(G)]
    peers += [dev(p, lax.rem(e + k, G), d) for k in range(1, G)]
    peers += [dev(p, e, lax.rem(d + k, Z)) for k in range(1, Z)]
    peers += [dev(after, e, d), dev(before, e, d)]
    for peer in peers:
        pl.semaphore_signal(barrier, inc=1, device_id=peer, device_id_type=pl.DeviceIdType.MESH)

    small[0].wait()
    ids = [idb_ref[k:k + 1, :].astype(F32) for k in range(2)]
    labels = lax.broadcasted_iota(jnp.int32, (8, T), 0).astype(F32)
    onehot = [jnp.where(ids[k] == labels, 1.0, 0.0) for k in range(2)]
    earlier = lax.broadcasted_iota(jnp.int32, (T, T), 0) < lax.broadcasted_iota(
        jnp.int32, (T, T), 1)
    earlier = jnp.where(earlier, 1.0, 0.0).astype(BF16)
    counts = [jnp.dot(onehot[k].astype(BF16), earlier, preferred_element_type=F32)
              for k in range(2)]
    counts[1] = counts[1] + jnp.sum(onehot[0], axis=1, keepdims=True)
    rank = [jnp.sum(counts[k] * onehot[k], axis=0, keepdims=True) for k in range(2)]
    shift = lax.rem(e * R, TILE).astype(F32)
    slots = lax.broadcasted_iota(jnp.int32, (W, T), 0).astype(F32)
    maps = []
    for g in range(G):
        pair = []
        for k in range(2):
            own = jnp.where((ids[k] >= g * L) & (ids[k] < (g + 1) * L),
                            shift + (ids[k] - g * L) * CAP + rank[k], -1.0)
            pair.append(jnp.where(slots == own, 1.0, 0.0).astype(BF16))
        maps.append(pair)
    both = jnp.concatenate([jnp.concatenate(pair, axis=1) for pair in maps], axis=0)

    spans = []
    at = 0
    for n in CHUNKS:
        spans.append((at, n))
        at += n
    assert at == U
    messages, fresh = message_plan(L * NA, L * NB)

    def units(ref, c):
        return ref.at[pl.ds(spans[c][0], spans[c][1])]

    def stage(c, g):
        return remote(units(gs.at[g], c), units(st.at[e], c), s_send.at[c, g], s_recv.at[c, e],
                      dev(mirror, g, d))

    def route(c):
        u, n = spans[c]
        cols = slice(u * LANES, (u + n) * LANES)
        picked = jnp.concatenate([dg_ref[:, 0, cols], dg_ref[:, 1, cols]], axis=0)
        placed = jnp.dot(both, picked, preferred_element_type=F32).astype(BF16)
        for g in range(G):
            for i in range(n):
                gs[g, u + i] = placed[g * W:(g + 1) * W, i * LANES:(i + 1) * LANES]

    def send_stage(c):
        for g in range(G):
            stage(c, g).start()

    bounds = [0, 2, 2 * N1, NTT] if QS > 1 else [0, 2, NTT]
    Q = len(bounds) - 1

    def rows_stage(q, g):
        span = pl.ds(bounds[q], bounds[q + 1] - bounds[q])
        return remote(ns.at[g, span], stn.at[e, span], n_send.at[q, g], n_recv.at[q, e],
                      dev(mirror, g, d))

    def send_rows(q):
        for g in range(G):
            rows_stage(q, g).start()

    def window(b):
        lo = b // 2 * 2 * DZ // LANES
        return range(lo, min(lo + NT, NTT))

    def place_of(t):
        return 2 * t if t < NTT // 2 else 2 * (NTT - 1 - t) + 1

    def rows_gather(i, r, to):
        return remote(nall.at[r, i], nall.at[r, i], nz_send.at[i, to], nz_recv.at[i, r],
                      dev(p, e, to))

    def rows_dests(i):
        return [b for b in range(1, Z - 1) if i in [place_of(t) for t in window(b)]]

    def combine_rows(q):
        for s in range(G):
            span = pl.ds(bounds[q], bounds[q + 1] - bounds[q])
            remote(ns.at[0, span], stn.at[s, span], n_send.at[q, 0], n_recv.at[q, s],
                   dev(mirror, 0, d)).wait_recv()
        for i in range(bounds[q], bounds[q + 1]):
            for row in range(0, FR, TILE):
                parts = [stn[s, i, row - starts[s]:row - starts[s] + TILE, :] for s in range(G)
                         if starts[s] <= row < starts[s] + W]
                nall[d, i, row:row + TILE, :] = functools.reduce(lambda a, b: a + b, parts)
            for to in rows_dests(i):
                @pl.when(d != to)
                def _():
                    rows_gather(i, d, to).start()

    def rows_arrive(i, r):
        rows_gather(i, r, 1).wait_recv()

    def wait_rows_sent():
        for q in range(Q):
            for g in range(G):
                rows_stage(q, g).wait_send()
        for i in range(NTT):
            for to in rows_dests(i):
                @pl.when(d != to)
                def _():
                    rows_gather(i, d, to).wait_send()

    def gather(c, r, to):
        return remote(units(gall.at[r], c), units(gall.at[r], c), z_send.at[c, to],
                      z_recv.at[c, r], dev(p, e, to))

    def combine(c):
        for s in range(G):
            remote(units(gs.at[0], c), units(st.at[s], c), s_send.at[c, 0], s_recv.at[c, s],
                   dev(mirror, 0, d)).wait_recv()
        u, n = spans[c]
        for v in range(u, u + n):
            for i in range(0, FR, TILE):
                parts = [st[s, v, i - starts[s]:i - starts[s] + TILE, :] for s in range(G)
                         if starts[s] <= i < starts[s] + W]
                gall[d, v, i:i + TILE, :] = functools.reduce(lambda a, b: a + b, parts)
        order = [Z - 2, 1] + list(range(2, Z - 2))
        for to in order:
            @pl.when((d != to) & first)
            def _():
                gather(c, d, to).start()
        order[0:2] = [1, Z - 2]
        for to in order:
            @pl.when((d != to) & (d > 0))
            def _():
                gather(c, d, to).start()

    def mask_into(lhs, at, row, n, height):
        whole = turned[pl.ds(pl.multiple_of(row, 8), n), 0:height]
        place = lax.rem(lax.broadcasted_iota(jnp.int32, (1, height), 1), R)
        for j in range(L):
            mine = (place >= j * CAP) & (place < (j + 1) * CAP)
            lhs[at + j * n:at + (j + 1) * n, :] = jnp.where(mine, whole, 0.0).astype(BF16)

    def turn(t, block):
        turned[t * LANES:(t + 1) * LANES, 0:block.shape[0]] = block.astype(F32).T

    def rows_for_end(q):
        at, n = [(0, NA), (L * NA, NB)][q]
        i = 2 * q + side

        @pl.when(is_adj)
        def _():
            for k in range(Z - 1):
                @pl.when(low + k != d)
                def _():
                    rows_arrive(i, low + k)
            turn(0, nall[pl.ds(low, Z - 1), i].reshape((Z - 1) * FR, LANES))
            mask_into(lhs_red, at, side * (LANES - n), n, (Z - 1) * FR)

    def rows_for_own():
        for b in range(1, Z - 1):
            @pl.when(d == b)
            def _():
                for t in window(b):
                    i = place_of(t)
                    early = b in (1, Z - 2) and i in range(int(b != 1), 2 * QS, 2)
                    for r in range(Z):
                        if r != b and not (early and r != (0 if b == 1 else Z - 1)):
                            rows_arrive(i, r)
                for k, t in enumerate(window(b)):
                    turn(k, nall[:, place_of(t)].reshape(Z * FR, LANES))
                mask_into(lhs_own, 0, own_row, DZ, Z * FR)
        for b in (0, Z - 1):
            @pl.when(d == b)
            def _():
                for k in range(N1):
                    t = k if b == 0 else NTT - N1 + k
                    turn(k, nall[b, place_of(t)])
                mask_into(lhs_end, 0, end_row, DZ, FR)

    def block_arrives(c, r):
        return gather(c, r, 1)

    def onto_end(m):
        u, n, lo, h = messages[m]
        at = (pl.ds(u, n), pl.ds(lo, h))
        return remote(ps.at[at], rp.at[at], r_send.at[m], r_recv.at[m], dev(p, e, end_dev))

    def reduce(m):
        u, n, lo, h = messages[m]

        @pl.when(is_adj)
        def _():
            for c in fresh[m]:
                for i in range(Z - 1):
                    @pl.when(low + i != d)
                    def _():
                        block_arrives(c, low + i).wait_recv()
            block = jnp.concatenate(
                [gall[pl.ds(low, Z - 1), u + i].reshape((Z - 1) * FR, LANES) for i in range(n)],
                axis=1)
            part = jnp.dot(lhs_red[lo:lo + h, :], block, preferred_element_type=F32).astype(BF16)
            for i in range(n):
                ps[u + i, lo:lo + h, :] = part[:, i * LANES:(i + 1) * LANES]
            onto_end(m).start()

    def own_wait(c):
        @pl.when(is_adj)
        def _():
            block_arrives(c, jnp.where(d == 1, 0, Z - 1)).wait_recv()
        if Z > 4:
            @pl.when(is_mid & jnp.logical_not(is_adj))
            def _():
                for r in range(Z):
                    @pl.when(d != r)
                    def _():
                        block_arrives(c, r).wait_recv()

    def own_term(u, n):
        cols = slice(u * LANES, (u + n) * LANES)

        @pl.when(is_mid)
        def _():
            block = jnp.concatenate(
                [gall[:, u + i].reshape(Z * FR, LANES) for i in range(n)], axis=1)
            whole = jnp.dot(lhs_own[...], block, preferred_element_type=F32)
            for j in range(L):
                grad_ref[j, :, cols] = whole[j * DZ:(j + 1) * DZ]

        @pl.when(is_end)
        def _():
            block = jnp.concatenate([gall[d, u + i] for i in range(n)], axis=1)
            whole = jnp.dot(lhs_end[...], block, preferred_element_type=F32)
            for j in range(L):
                grad_ref[j, :, cols] = whole[j * DZ:(j + 1) * DZ]

    def add_part(m):
        u, n, lo, h = messages[m]

        @pl.when(is_end)
        def _():
            onto_end(m).wait_recv()
            for i in range(u, u + n):
                cols = slice(i * LANES, (i + 1) * LANES)
                for at, size, row in ((0, NA, side * NB), (L * NA, NB, (1 - side) * NA)):
                    if size and lo <= at < lo + h:
                        for j in range(L):
                            rows_of = pl.ds(pl.multiple_of(row, 8), size)
                            grad_ref[j, rows_of, cols] += rp[
                                i, at + j * size:at + (j + 1) * size].astype(F32)

    def forward_tokens():
        for copy in small[3:]:
            copy.wait()
        tokens = tok_ref[...].astype(F32)
        inv = lax.rsqrt(jnp.mean(tokens * tokens, axis=-1, keepdims=True) + 1e-05)
        normed = (tokens * inv * gain_ref[...]).astype(BF16)
        logits = lax.dot_general(normed, router_ref[...], (((1,), (1,)), ((), ())),
                                 preferred_element_type=F32)
        lane_e = lax.broadcasted_iota(jnp.int32, logits.shape, 1).astype(F32)
        diagonal = lax.broadcasted_iota(jnp.int32, (T, T), 0) == lax.broadcasted_iota(
            jnp.int32, (T, T), 1)
        one, two = [
            jnp.sum(jnp.where(diagonal, idf_ref[k:k + 1, :].astype(F32), 0.0), axis=1,
                    keepdims=True)
            for k in range(2)]
        l0 = jnp.sum(jnp.where(lane_e == one, logits, 0.0), axis=1, keepdims=True)
        l1 = jnp.sum(jnp.where(lane_e == two, logits, 0.0), axis=1, keepdims=True)
        lane = lax.broadcasted_iota(jnp.int32, (T, LANES), 1).astype(F32)
        xall[0] = normed
        call[0] = jnp.where(lane == one, jax.nn.sigmoid(l0 - l1), 0.0) + jnp.where(
            lane == two, jax.nn.sigmoid(l1 - l0), 0.0)
        for copy in tokens_out:
            copy.start()

    tokens_out = []
    for k in range(1, G):
        to = dev(p, lax.rem(e + k, G), d)
        tokens_out += [remote(xall.at[0], xall.at[k], x_send.at[k], x_recv.at[k], to),
                       remote(call.at[0], call.at[k], c_send.at[k], c_recv.at[k], to)]

    def tokens_in():
        for copy in tokens_out:
            copy.wait_recv()

    def widen(j, c):
        if c == 0:
            weights[j][0].wait()
            weights[j][1].wait()
        n = HID // BLOCKS
        cols = slice(c * n, (c + 1) * n)
        block = xall[...].reshape(G * T, D)
        gate = jnp.dot(block, wg[j, :, cols], preferred_element_type=F32)
        up = jnp.dot(block, wu[j, :, cols], preferred_element_type=F32)
        hid[:, cols] = (jax.nn.gelu(gate) * up).astype(BF16)

    def narrow(j):
        weights[j][2].wait()
        weight = call[...].reshape(G * T, LANES)
        lanes = lax.broadcasted_iota(jnp.int32, (G * T, LANES), 1)
        weight = jnp.sum(jnp.where(lanes == e * L + j, weight, 0.0), axis=1, keepdims=True)
        for c in range(BLOCKS):
            cols = slice(c * (D // BLOCKS), (c + 1) * (D // BLOCKS))
            out = jnp.dot(hid[...], wd[j, :, cols], preferred_element_type=F32)
            out = weight * out.astype(BF16).astype(F32)
            if j == 0:
                acc[:, cols] = out
            else:
                acc[:, cols] += out

    back = []
    for k in range(1, G):
        back.append(remote(po.at[k], pi.at[k], p_send.at[k], p_recv.at[k],
                           dev(p, lax.rem(e + G - k, G), d)))
    onward = remote(mixed, landed, h_sem.at[0], h_sem.at[1], dev(after, e, d))

    def give_back():
        for k in range(1, G):
            po[k] = acc[k * T:(k + 1) * T, :].astype(BF16)
            back[k - 1].start()

    def hand_on():
        total = tok_ref[...].astype(F32) + acc[0:T, :]
        for k, copy in enumerate(back):
            copy.wait_recv()
            total = total + pi[k + 1].astype(F32)
        mixed[...] = total.astype(BF16)
        onward.start()

    C = len(spans)

    def sent(c):
        for g in range(G):
            stage(c, g).wait_send()
        for to in range(1, Z - 1):
            @pl.when(d != to)
            def _():
                gather(c, d, to).wait_send()

    def parts_sent():
        @pl.when(is_adj)
        def _():
            for m in range(len(messages)):
                onto_end(m).wait_send()

    def route_rows():
        small[2].wait()
        for g in range(G):
            placed = jnp.dot(maps[g][0] + maps[g][1], nb_ref[...],
                             preferred_element_type=F32).astype(BF16)
            for t in range(NTT):
                ns[g, place_of(t)] = placed[:, t * LANES:(t + 1) * LANES]

    def out(c):
        route(c)
        send_stage(c)

    M = len(messages)
    extra = M - C

    small[1].wait()
    route(0)
    pl.semaphore_wait(barrier, len(peers))
    send_stage(0)
    route_rows()
    send_rows(0)
    weights = []
    for j in range(L):
        trio = [local(wg_hbm.at[j], wg.at[j], w_sem.at[j, 0]),
                local(wu_hbm.at[j], wu.at[j], w_sem.at[j, 1]),
                local(wd_hbm.at[j], wd.at[j], w_sem.at[j, 2])]
        for copy in trio:
            copy.start()
        weights.append(trio)

    out(1)
    if QS > 1:
        send_rows(1)
    out(2)
    out(3)
    out(4)
    out(5)
    combine(0)
    forward_tokens()
    combine_rows(0)
    out(6)
    out(7)
    send_rows(Q - 1)
    combine(1)
    if QS > 1:
        combine_rows(1)
    combine(2)
    rows_for_end(0)
    reduce(0)
    combine(3)
    reduce(1)
    if QS > 1:
        rows_for_end(1)
        reduce(2)
    combine(4)
    reduce(2 + extra)
    tokens_in()
    widen(0, 0)
    combine(5)
    reduce(3 + extra)
    widen(0, 1)
    widen(0, 2)
    combine(6)
    reduce(4 + extra)
    narrow(0)
    if L > 1:
        widen(1, 0)
    combine(7)
    reduce(5 + extra)
    if L > 1:
        widen(1, 1)
        widen(1, 2)
    reduce(6 + extra)
    if L > 1:
        narrow(1)
    give_back()
    combine_rows(Q - 1)
    rows_for_own()
    reduce(7 + extra)
    hand_on()
    for c in range(C):
        own_wait(c)
    for u in range(0, U, 2):
        own_term(u, 2)
    for c in range(C):
        sent(c)
    wait_rows_sent()
    for copy in tokens_out + back:
        copy.wait_send()
    onward.wait_recv()
    ho_ref[...] = landed[...]
    onward.wait_send()
    for m in range(M):
        add_part(m)
    parts_sent()


def write_out(handed_ref, grad_ref, handed_hbm, grad_hbm, sem):
    L, DZ = grad_ref.shape[:2]
    half = DZ // 2
    copies = [pltpu.make_async_copy(handed_ref, handed_hbm, sem.at[0])]
    for j in range(L):
        for i in range(2):
            at = (j, pl.ds(i * half, half))
            copies.append(pltpu.make_async_copy(
                grad_ref.at[at], grad_hbm.at[at], sem.at[1 + 2 * j + i]))
    for copy in copies:
        copy.start()
    for copy in copies:
        copy.wait()


def shards(
    acts_fwd, ids_fwd, norm_gain, router_w, gate_w, up_w, down_w, normed_bwd, ids_bwd, dgate_bwd
):
    S, G, Z = lax.axis_size("pipe"), lax.axis_size("expert"), lax.axis_size("dp")
    L = gate_w.shape[1]
    E = G * L
    T, D = acts_fwd.shape[2:]
    HID = gate_w.shape[3]
    U = HID // LANES
    C = len(CHUNKS)
    DZ = D // Z
    R = L * CAP
    FR = G * R
    W = max(-(-(s + 1) * R // TILE) * TILE - s * R // TILE * TILE for s in range(G))
    NTT = D // LANES
    N1, NT = window_sizes(D, Z)
    M = len(message_plan(L * min(DZ, LANES), L * (DZ - min(DZ, LANES)))[0])
    vmem = pl.BlockSpec(memory_space=pltpu.VMEM)
    hbm = pl.BlockSpec(memory_space=pltpu.HBM)
    dma = pltpu.SemaphoreType.DMA
    V = pltpu.VMEM
    handed, grad = pl.pallas_call(
        functools.partial(relay_kernel, (S, G, Z, L)),
        out_shape=(jax.ShapeDtypeStruct((T, D), BF16), jax.ShapeDtypeStruct((L, DZ, HID), F32)),
        in_specs=[hbm] * 10,
        out_specs=(vmem, vmem),
        scratch_shapes=[
            V((T, D), BF16), V((2, T), jnp.int32), V((1, D), F32), V((E, D), BF16),
            V((T, D), BF16), V((2, T), jnp.int32), V((T, 2, HID), BF16), dma((7,)),
            V((L, D, HID), BF16), V((L, D, HID), BF16), V((L, HID, D), BF16),
            V((G, U, W, LANES), BF16), V((G, U, W, LANES), BF16), V((Z, U, FR, LANES), BF16),
            V((G, NTT, W, LANES), BF16), V((G, NTT, W, LANES), BF16),
            V((Z, NTT, FR, LANES), BF16), V((NT * LANES, Z * FR), F32),
            V((L * DZ, (Z - 1) * FR), BF16), V((L * DZ, Z * FR), BF16), V((L * DZ, FR), BF16),
            V((U, L * DZ, LANES), BF16), V((U, L * DZ, LANES), BF16),
            V((G, T, D), BF16), V((G, T, LANES), F32), V((G * T, HID), BF16), V((G * T, D), F32),
            V((G, T, D), BF16), V((G, T, D), BF16), V((T, D), BF16), V((T, D), BF16),
            dma((L, 3)), dma((C, G)), dma((C, G)), dma((3, G)), dma((3, G)), dma((NTT, Z)), dma((NTT, Z)),
            dma((C, Z)), dma((C, Z)), dma((M,)), dma((M,)),
            dma((G,)), dma((G,)), dma((G,)), dma((G,)), dma((G,)), dma((G,)), dma((2,)),
        ],
        compiler_params=pltpu.CompilerParams(
            collective_id=0, has_side_effects=True, vmem_limit_bytes=36 << 20),
    )(*(pltpu.with_memory_space_constraint(x, pltpu.HBM) for x in (
        acts_fwd[0, 0], ids_fwd[0, 0].T, norm_gain, router_w[0].T, gate_w[0], up_w[0], down_w[0],
        normed_bwd[0, 0], ids_bwd[0, 0].T, dgate_bwd[0, 0],
    )))
    handed, grad = pl.pallas_call(
        write_out,
        out_shape=(jax.ShapeDtypeStruct((T, D), BF16), jax.ShapeDtypeStruct((L, DZ, HID), F32)),
        in_specs=[vmem] * 2,
        out_specs=[pl.BlockSpec(memory_space=pl.ANY)] * 2,
        scratch_shapes=[dma((1 + 2 * L,))],
        compiler_params=pltpu.CompilerParams(vmem_limit_bytes=1 << 20),
    )(handed, grad)
    return handed[None, None], grad[None]


def solution(mesh):
    in_specs = (
        P("pipe", "dp", "expert", None),
        P("pipe", "dp", "expert", None),
        P("pipe", None),
        P("pipe", None, None),
        P("pipe", "expert", None, None),
        P("pipe", "expert", None, None),
        P("pipe", "expert", None, None),
        P("pipe", "dp", "expert", None),
        P("pipe", "dp", "expert", None),
        P("pipe", "dp", "expert", None, None),
    )
    out_specs = (P("pipe", "dp", "expert", None), P("pipe", "expert", "dp", None))
    return jax.shard_map(shards, mesh=mesh, in_specs=in_specs, out_specs=out_specs, check_vma=False)
```
